256 devices in a mesh: seed: 2 (over core), px: 16 (over y_lo, z), py: 8 (over x, y_hi).
Axes of the slice: x: 4, y: 4 (y_hi: 2, y_lo: 2; y = y_hi * 2 + y_lo), z: 8, core: 2. Of those that a mesh axis runs over, the one named last changes fastest.
Arguments:
- input_field: float32 [1, 3, 128, 128, 128], P(None, None, 'px', 'py'), may hold values from -6 to 6
- target_field: float32 [1, 3, 128, 128, 128], P(None, None, 'px', 'py'), may hold values from -6 to 6
- row_mask: int32 [256, 128], P(('seed', 'px'), 'py'), parts along dimension 0, may hold values from 0 to 2
- modes: int32 [6, 32], P('seed'), parts along dimension 0, may hold values from 0 to 127, as said below
- lift_weight: float32 [64, 3], P('seed'), parts along dimension 0, may hold values from -3.5 to 3.5
- mix_weight: float32 [64, 32], P('seed'), parts along dimension 0, may hold values from -1 to 1
- spectral_weight: float32 [4, 32, 32, 32, 1024], P('seed', 'py', None, 'px'), parts along dimension 0, may hold values from -8 to 8
- proj_weight: float32 [6, 32], P('seed'), parts along dimension 0, may hold values from -1 to 1
Outputs:
- lift_grad: float32 [64, 3], P('seed'), parts along dimension 0
- mix_grad: float32 [64, 32], P('seed'), parts along dimension 0
- proj_grad: float32 [6, 32], P('seed'), parts along dimension 0
- spectral_grad: float32 [4, 32, 32, 32, 1024], P('seed', 'py', None, 'px'), parts along dimension 0
The draws below stay inside these ranges and needn't reach their ends.
There are 2 independent parts, one for each index of `seed`. The reference program is written for one: setup_inputs(seed, part) draws one part's arguments, and reference() takes and returns one part's arrays. A program takes and returns all parts, laid end to end along the dimension named above; an argument that names none is the same for every part. Nothing has to cross between parts.
Inputs may be any that keep to these rules, and one draw needn't show every extreme that they name: `modes`: each row holds the usual Fourier neural operator truncation of one grid dimension: the frequencies 0 .. 15 and 112 .. 127, each once, in an order drawn from the seed.
All inputs are finite; a program needn't handle non-finite values.
Results may differ from the reference program's by a relative error of at most 0.00021.
Values sent between devices are 32-bit elements; how exact they have to be, the bound alone decides.
No kernel may reach another device: no remote copies, remote signals or barrier semaphores. Data moves between devices by JAX's collectives and lax.ppermute only.
A program may use at most 128 MiB of HBM per device.

```python
import math
import jax
import jax.numpy as jnp
from jax import lax

B = 1
C = 32
N = 128
M = 32


def draw_modes(key, part):
    half_count = M // 2
    lowest = jnp.arange(half_count, dtype=jnp.int32)
    kept = jnp.concatenate([lowest, lowest + (N - half_count)])
    rows_list = []
    for axis_number in range(3):
        order = jax.random.permutation(jax.random.fold_in(key, 11 + axis_number), M)
        rows_list.append(kept[order].astype(jnp.int32))
    return jnp.stack(rows_list)


def set_ends(entries, rng, low, high):
    longest = entries.shape.index(max(entries.shape))
    spots = []
    for shift in (0, 1):
        where = [jax.random.randint(jax.random.fold_in(rng, axis), (), 0, length) for axis, length in enumerate(entries.shape)]
        where[longest] = (where[longest] + shift) % entries.shape[longest]
        spots.append(tuple(where))
    return entries.at[spots[0]].set(low).at[spots[1]].set(high)


def steps_of(rng, dims, cuts, least, top_value):
    factor_of, own = 1.0, jax.random.fold_in(rng, 6)
    for position, parts in cuts:
        steps = jnp.exp(jax.random.uniform(jax.random.fold_in(own, position), (parts,), jnp.float32, least / len(cuts), top_value / len(cuts)))
        factor_of = factor_of * jnp.repeat(steps, dims[position] // parts).reshape([-1 if axis == position else 1 for axis in range(len(dims))])
    return factor_of


def gaussian(stream_key, shape, spread, bound, cuts=(), held_as=jnp.bfloat16):
    values = spread * jax.random.normal(stream_key, shape, jnp.float32)
    if cuts:
        values = values * steps_of(stream_key, shape, cuts, -0.22, 0.18)
    return jnp.clip(values, -bound, bound).astype(held_as)


def setup_inputs(seed: int = 0, part: int = 0) -> dict:
    key_of = jax.random.split(jax.random.key(seed), 9)
    own_keys = jax.random.split(jax.random.fold_in(key_of[8], part), 9)
    return {
        "input_field": gaussian(key_of[0], (B, 3, N, N, N), 1.0, 6.0, ((2, 16), (3, 8)), jnp.float32),
        "target_field": gaussian(key_of[1], (B, 3, N, N, N), 1.0, 6.0, ((2, 16), (3, 8)), jnp.float32),
        "row_mask": set_ends(jax.random.randint(own_keys[2], (N, N), 0, 3), jax.random.fold_in(own_keys[2], 1), 0, 2).astype(jnp.int32),
        "modes": draw_modes(jax.random.fold_in(jax.random.fold_in(key_of[8], part), 71), part),
        "lift_weight": gaussian(own_keys[4], (C, 3), 3 ** -0.5, 3.5, (), jnp.float32),
        "mix_weight": gaussian(own_keys[5], (C, C), C ** -0.5, 1.0, (), jnp.float32),
        "spectral_weight": gaussian(own_keys[6], (2, M, M, M, C * C), 1.4, 8.0, ((1, 8), (3, 16)), jnp.float32),
        "proj_weight": gaussian(own_keys[7], (3, C), C ** -0.5, 1.0, (), jnp.float32),
    }


HIGHEST = lax.Precision.HIGHEST

def contract(pattern, left, right):
    return jnp.einsum(pattern, left, right, precision=HIGHEST)

def tables(frequency, length):
    places = jnp.arange(length, dtype=jnp.int32)
    turn_count = places[:, None] * frequency.astype(jnp.int32)[None, :] % length
    angles = turn_count.astype(jnp.float32) * jnp.float32(2.0 * math.pi / length)
    return (jnp.cos(angles), jnp.sin(angles))

def rotate(halves, cosine, sine, direction, pattern):
    real_part = contract(pattern, halves[0], cosine) - direction * contract(pattern, halves[1], sine)
    imag_part = contract(pattern, halves[1], cosine) + direction * contract(pattern, halves[0], sine)
    return jnp.stack([real_part, imag_part])

def spectrum_of(fields, waves):
    x_cos, x_sin, y_cos, y_sin, z_cos, z_sin = waves
    along_z = jnp.stack([contract('kxyn,nm->kxym', fields, z_cos), -contract('kxyn,nm->kxym', fields, z_sin)])
    along_x = rotate(along_z, x_cos, x_sin, -1.0, 'kxyq,xm->kmyq')
    return rotate(along_x, y_cos, y_sin, -1.0, 'kpyq,ym->kpmq')

def field_of(spectrum, waves, scaling):
    x_cos, x_sin, y_cos, y_sin, z_cos, z_sin = waves
    along_y = rotate(spectrum, y_cos, y_sin, 1.0, 'kpmq,ym->kpyq')
    along_x = rotate(along_y, x_cos, x_sin, 1.0, 'kmyq,xm->kxyq')
    return scaling * (contract('kxyq,nq->kxyn', along_x[0], z_cos) - contract('kxyq,nq->kxyn', along_x[1], z_sin))

def mix_modes(flat_weights, spectrum):
    weights = flat_weights.reshape(flat_weights.shape[:4] + (C, C))
    real_part = contract('ipmq,pmqio->opmq', spectrum[0], weights[0]) - contract('ipmq,pmqio->opmq', spectrum[1], weights[1])
    imag_part = contract('ipmq,pmqio->opmq', spectrum[1], weights[0]) + contract('ipmq,pmqio->opmq', spectrum[0], weights[1])
    return jnp.stack([real_part, imag_part])

def sample_loss(params, sample, target, weights_mask, waves):
    lift_weight, mix_weight, spectral_weight, proj_weight = params
    lifted = contract('cj,jxyn->cxyn', lift_weight, sample)
    lifted_modes = spectrum_of(lifted, waves)
    spectral = field_of(mix_modes(spectral_weight, lifted_modes), waves, 1.0 / float(N ** 3))
    preact = contract('cd,dxyn->cxyn', mix_weight, lifted) + spectral
    output_field = contract('jc,cxyn->jxyn', proj_weight, jax.nn.gelu(preact))
    misfit = output_field - target
    return jnp.sum(weights_mask[None, :, :, None] * misfit * misfit)

def reference(input_field, target_field, row_mask, modes, lift_weight, mix_weight, spectral_weight, proj_weight):
    waves = tables(modes[0], N) + tables(modes[1], N) + tables(modes[2], N)
    weights_mask = row_mask.astype(jnp.float32)
    params = (lift_weight, mix_weight, spectral_weight, proj_weight)
    grad_fn = jax.grad(sample_loss)

    def accumulate(carry, pieces):
        grads = grad_fn(params, pieces[0], pieces[1], weights_mask, waves)
        return (jax.tree.map(jnp.add, carry, grads), None)
    zeros = jax.tree.map(jnp.zeros_like, params)
    totals, unused = lax.scan(accumulate, zeros, (input_field, target_field))
    cells = float(N ** 3)
    return (totals[0] / cells, totals[1] / cells, totals[3] / cells, totals[2])
```

```python
import math

import jax
import jax.numpy as jnp
from jax import lax
from jax.sharding import PartitionSpec as P

C = 32
N = 128
M = 32


HIGHEST = lax.Precision.HIGHEST


def contract(pattern, left, right):
    return jnp.einsum(pattern, left, right, precision=HIGHEST)


def tables(frequency, length):
    places = jnp.arange(length, dtype=jnp.int32)
    turn_count = places[:, None] * frequency[None, :] % length
    angles = turn_count.astype(jnp.float32) * jnp.float32(2.0 * math.pi / length)
    return (jnp.cos(angles), jnp.sin(angles))


def forward(fields, waves):
    x_cos, x_sin, y_cos, y_sin, z_cos, z_sin = waves
    count, depth, x_local, y_local, length = fields.shape
    real_z = contract("bkxyn,nr->rbxyk", fields, z_cos)
    imag_z = -contract("bkxyn,nr->rbxyk", fields, z_sin)
    along_z = jnp.stack([real_z, imag_z], axis=2).reshape((M, count, 2, x_local, y_local * depth))

    def along_y(pieces):
        shape_now = pieces.shape
        split = pieces.reshape(shape_now[:4] + (N, depth))
        real_part = split[:, :, 0]
        imag_part = split[:, :, 1]
        new_real = contract("rbpyk,yq->rbpqk", real_part, y_cos) + contract(
            "rbpyk,yq->rbpqk", imag_part, y_sin
        )
        new_imag = contract("rbpyk,yq->rbpqk", imag_part, y_cos) - contract(
            "rbpyk,yq->rbpqk", real_part, y_sin
        )
        return jnp.stack([new_real, new_imag], axis=2)

    pieces = lax.all_to_all(along_z, "px", split_axis=0, concat_axis=3, tiled=True)
    real_part = pieces[:, :, 0]
    imag_part = pieces[:, :, 1]
    new_real = contract("rbxK,xp->rbpK", real_part, x_cos) + contract(
        "rbxK,xp->rbpK", imag_part, x_sin
    )
    new_imag = contract("rbxK,xp->rbpK", imag_part, x_cos) - contract(
        "rbxK,xp->rbpK", real_part, x_sin
    )
    first_pass = jnp.stack([new_real, new_imag], axis=2)
    return along_y(lax.all_to_all(first_pass, "py", split_axis=3, concat_axis=4, tiled=True))


def inverse(spectrum, waves, scaling, y_local):
    x_cos, x_sin, y_cos, y_sin, z_cos, z_sin = waves
    r_local, count, two, p_local, q_count, depth = spectrum.shape
    real_part = spectrum[:, :, 0]
    imag_part = spectrum[:, :, 1]
    real_y = contract("rbpqk,yq->rbpyk", real_part, y_cos) - contract(
        "rbpqk,yq->rbpyk", imag_part, y_sin
    )
    imag_y = contract("rbpqk,yq->rbpyk", imag_part, y_cos) + contract(
        "rbpqk,yq->rbpyk", real_part, y_sin
    )
    along_y = jnp.stack([real_y, imag_y], axis=2).reshape((r_local, count, 2, p_local, N * depth))
    pieces = lax.all_to_all(along_y, "py", split_axis=4, concat_axis=3, tiled=True)
    real_in = pieces[:, :, 0]
    imag_in = pieces[:, :, 1]
    new_real = contract("rbpK,xp->rbxK", real_in, x_cos) - contract("rbpK,xp->rbxK", imag_in, x_sin)
    new_imag = contract("rbpK,xp->rbxK", imag_in, x_cos) + contract("rbpK,xp->rbxK", real_in, x_sin)
    second_pass = jnp.stack([new_real, new_imag], axis=2)
    pieces = lax.all_to_all(second_pass, "px", split_axis=3, concat_axis=0, tiled=True)
    shape_now = pieces.shape
    split = pieces.reshape(shape_now[:4] + (y_local, depth))
    return scaling * (
        contract("rbxyk,nr->bkxyn", split[:, :, 0], z_cos)
        - contract("rbxyk,nr->bkxyn", split[:, :, 1], z_sin)
    )


def unfold(flat_weights):
    return flat_weights.reshape(flat_weights.shape[:4] + (C, C))


def mix_modes(weights, spectrum):
    first = spectrum[:, :, 0]
    second = spectrum[:, :, 1]
    real_part = contract("rbpqi,pqrio->rbpqo", first, weights[0]) - contract(
        "rbpqi,pqrio->rbpqo", second, weights[1]
    )
    imag_part = contract("rbpqi,pqrio->rbpqo", second, weights[0]) + contract(
        "rbpqi,pqrio->rbpqo", first, weights[1]
    )
    return jnp.stack([real_part, imag_part], axis=2)


def mix_back(weights, spectrum, incoming):
    first = spectrum[:, :, 0]
    second = spectrum[:, :, 1]
    grad_real = incoming[:, :, 0]
    grad_imag = incoming[:, :, 1]
    weight_real = contract("rbpqi,rbpqo->pqrio", first, grad_real) + contract(
        "rbpqi,rbpqo->pqrio", second, grad_imag
    )
    weight_imag = contract("rbpqi,rbpqo->pqrio", first, grad_imag) - contract(
        "rbpqi,rbpqo->pqrio", second, grad_real
    )
    modes_real = contract("rbpqo,pqrio->rbpqi", grad_real, weights[0]) + contract(
        "rbpqo,pqrio->rbpqi", grad_imag, weights[1]
    )
    modes_imag = contract("rbpqo,pqrio->rbpqi", grad_imag, weights[0]) - contract(
        "rbpqo,pqrio->rbpqi", grad_real, weights[1]
    )
    return (jnp.stack([weight_real, weight_imag]), jnp.stack([modes_real, modes_imag], axis=2))


def total(value):
    flat = value.reshape((1, -1))
    copies = jnp.broadcast_to(flat, (128,) + flat.shape[1:])
    pieces = lax.all_to_all(copies, ("px", "py"), split_axis=0, concat_axis=0, tiled=True)
    return jnp.sum(pieces, axis=0)


def body(
    input_field,
    target_field,
    row_mask,
    modes,
    lift_weight,
    mix_weight,
    spectral_weight,
    proj_weight,
):
    waves = tables(modes[0], N) + tables(modes[1], N) + tables(modes[2], N)
    cells = float(N**3)
    y_local = input_field.shape[3]
    square_weights = unfold(spectral_weight)
    input_modes = forward(input_field, waves)
    lifted_modes = contract("cj,rbtpqj->rbtpqc", lift_weight, input_modes)
    spectral = inverse(mix_modes(square_weights, lifted_modes), waves, 1.0 / cells, y_local)
    pointwise = contract("cd,dj->cj", mix_weight, lift_weight)
    preact = contract("cj,bjxyn->bcxyn", pointwise, input_field) + spectral
    active, gelu_back = jax.vjp(jax.nn.gelu, preact)
    output_field = contract("jc,bcxyn->bjxyn", proj_weight, active)
    weights_mask = row_mask.astype(jnp.float32)[None, None, :, :, None]
    out_grad = 2.0 * weights_mask * (output_field - target_field)
    proj_grad = contract("bjxyn,bcxyn->jc", out_grad, active)
    preact_grad = gelu_back(contract("jc,bjxyn->bcxyn", proj_weight, out_grad))[0]
    cross = contract("bcxyn,bjxyn->cj", preact_grad, input_field)
    mixed_grad = forward(preact_grad, waves) / cells
    square_grad, modes_grad = mix_back(square_weights, lifted_modes, mixed_grad)
    spectral_grad = square_grad.reshape(spectral_weight.shape)
    lift_part = contract("rbtpqc,rbtpqj->cj", modes_grad, input_modes)
    sums = total(jnp.concatenate([cross.reshape(-1), lift_part.reshape(-1), proj_grad.reshape(-1)]))
    cross = sums[:96].reshape(C, 3)
    lift_total = contract("dc,dj->cj", mix_weight, cross) + sums[96:192].reshape(C, 3)
    mix_total = contract("cj,dj->cd", cross, lift_weight)
    proj_total = sums[192:].reshape(3, C)
    return (lift_total / cells, mix_total / cells, proj_total / cells, spectral_grad)


def solution(mesh):
    in_specs = (
        P(None, None, "px", "py", None),
        P(None, None, "px", "py", None),
        P(("seed", "px"), "py"),
        P("seed", None),
        P("seed", None),
        P("seed", None),
        P("seed", "py", None, "px", None),
        P("seed", None),
    )
    out_specs = (
        P("seed", None),
        P("seed", None),
        P("seed", None),
        P("seed", "py", None, "px", None),
    )
    return jax.shard_map(body, mesh=mesh, in_specs=in_specs, out_specs=out_specs, check_vma=False)
```

```python
import math

import jax
import jax.numpy as jnp
from jax import lax
from jax.experimental import pallas as pl
from jax.experimental.pallas import tpu as pltpu
from jax.sharding import PartitionSpec as P

C = 32
N = 128
M = 32
F32 = jnp.float32
BF16 = jnp.bfloat16
SCALE = 1.0 / float(N**3)
GELU_A = math.sqrt(2.0 / math.pi)
GELU_B = 0.044715

NN = (((1,), (0,)), ((), ()))
NT = (((1,), (1,)), ((), ()))


def split(value):
    high = value.astype(BF16)
    return high, (value - high.astype(F32)).astype(BF16)


def mul(left, right, dims):
    return lax.dot_general(left, right, dims, preferred_element_type=F32)


def dot3(left, right, dims=NN):
    left_high, left_low = left if isinstance(left, tuple) else split(left)
    right_high, right_low = right if isinstance(right, tuple) else split(right)
    return (
        mul(left_low, right_high, dims)
        + mul(left_high, right_low, dims)
        + mul(left_high, right_high, dims)
    )


def iota(shape, axis):
    return lax.broadcasted_iota(jnp.int32, shape, axis)


def wave(turns):
    place = jnp.abs((turns & (N - 1)) - N // 2).astype(F32)
    angle = (place - N / 4) * (2.0 * math.pi / N)
    square = angle * angle
    series = 1.0 / 39916800.0
    for term in (362880.0, 5040.0, 120.0, 6.0, 1.0):
        series = 1.0 / term - square * series
    return angle * series


def regroup(pieces):
    group = iota(pieces[0].shape, 1) // 16
    out = []
    for target in range(8):
        total = pieces[target]
        for source in range(8):
            if source != target:
                moved = pltpu.roll(pieces[source], (16 * (source - target)) % 128, 1)
                total = jnp.where(group == source, moved, total)
        out.append(total)
    return out


def depth_waves(freq_ref):
    shape = (N, 128)
    lane = iota(shape, 1)
    return wave(iota(shape, 0) * freq_ref[2:3, :] + 32 * (lane & 1))


def input_depth(freq_ref, field_ref, out_ref):
    table = split(depth_waves(freq_ref).T[:64])
    lane = iota((32, 128), 1)
    blank = jnp.zeros((16, N), F32)
    for x in range(8):
        rows = [field_ref[channel, x] for channel in range(3)] + [blank]
        both = jnp.concatenate(rows + rows, axis=0)
        result = dot3(table, both, NT)
        out_ref[pl.ds(x, 32, stride=8), :] = jnp.where(lane < 64, result[:32], result[32:])


def rows_waves(freq_row, phase):
    shape = (256, 128)
    row = iota(shape, 0)
    place = (row // 16) * 8 + row % 8
    return place * freq_row + phase(row // 8 % 2)


def input_rows(freq_ref, pieces_ref, out_ref):
    lane = iota((256, 128), 1)
    table = wave(rows_waves(freq_ref[4:5, :], lambda part: 32 * ((lane // 4) % 2 - part)))
    out_ref[...] = dot3(table.T[:64], pieces_ref[...])


def mix_kernel(freq_ref, pieces_ref, lift_ref, weight_ref, modes_ref, out_ref, held_ref):
    pieces = [pieces_ref[8 * source : 8 * source + 8, :] for source in range(8)]
    group = iota((8, 128), 1) // 16
    rows = jnp.concatenate(regroup(pieces), axis=0)
    shape = (N, 128)
    lane = iota(shape, 1)
    turns = iota(shape, 0) * freq_ref[1:2, :]
    left = wave(turns + 32 * (lane // 64))
    right = wave(turns + 32 * (lane // 64) - 32)
    rows = split(rows)
    held_ref[:, :128] = dot3(rows, left)
    held_ref[:, 128:] = dot3(rows, right)
    even = iota((4, 128), 1) % 2 == 0
    modes_ref[...] = jnp.zeros((32, 128), F32)
    for channel in range(3):
        both = []
        for parity in range(2):
            base = 8 * (4 * parity + channel)
            both.append(held_ref[base : base + 4, :128] + held_ref[base + 4 : base + 8, 128:])
        modes_ref[pl.ds(channel, 4, stride=8), :] = jnp.where(even, both[0], both[1])
    lift = split(lift_ref[...])
    fold = jnp.where(iota((32, 1024), 0) == iota((32, 1024), 1) % 32, SCALE, 0.0).astype(BF16)
    for p in range(4):
        spread = dot3(modes_ref[8 * p : 8 * p + 8, :].T, lift)
        real, imag = spread[:64], spread[64:]
        first, second = weight_ref[0, p], weight_ref[1, p]
        product = jnp.concatenate([first * real - second * imag, second * real + first * imag], axis=0)
        high, low = split(product)
        mixed = mul(fold, low, NT) + mul(fold, high, NT)
        for target in range(8):
            start = 8 * (target // 2)
            out_ref[target, p] = mixed[start : start + 8]


def expand(freq_ref, pieces_ref, out_ref, held_ref):
    shape = (256, 128)
    row, lane = iota(shape, 0), iota(shape, 1)
    table = wave((row % 128) * freq_ref[1:2, :] + 32 * (lane // 64 - row // 128))
    table = jnp.where(freq_ref[3:4, :] == 1, table, 0.0)
    result = dot3(pieces_ref[...], table, NT)
    held_ref[:256, :] = result[:, :128]
    held_ref[256:, :] = result[:, 128:]
    parts = []
    for part in range(2):
        pieces = [held_ref[pl.ds(256 * part + o, 32, stride=8), :] for o in range(8)]
        parts.append(regroup(pieces))
    table = split(wave(rows_waves(freq_ref[0:1, :], lambda part: 32 * (lane // 32 - part)))[:, :64])
    for pair in range(4):
        wide = jnp.concatenate(
            [
                jnp.concatenate([parts[part][2 * pair + k] for part in range(2)], axis=0)
                for k in range(2)
            ],
            axis=1,
        )
        result = dot3(table, wide)
        for k in range(2):
            start = 256 * (2 * pair + k)
            out_ref[start : start + 256, :] = result[:, 128 * k : 128 * k + 128]


def grid_kernel(
    freq_ref, pieces_ref, field_ref, target_ref, mask_ref, point_ref, proj_ref, out_ref, small_ref,
    point_grad, proj_grad,
):
    waves = depth_waves(freq_ref).T[:64]
    point = point_ref[...]
    proj = split(proj_ref[...])
    blank = jnp.zeros((16, N), F32)
    empty = jnp.zeros((64, N), F32)
    point_grad[...] = jnp.zeros_like(point_grad)
    proj_grad[...] = jnp.zeros_like(proj_grad)

    def plane(x, carry):
        rows = [field_ref[channel, x] for channel in range(3)] + [blank]
        stack = jnp.concatenate([waves] + rows, axis=0)
        aims = [target_ref[channel, x] for channel in range(3)] + [blank, empty]
        aim = jnp.concatenate(aims, axis=0).T
        coefs = [pieces_ref[pl.ds(512 * o + x, 64, stride=8), :] for o in range(4)]
        coefs = jnp.concatenate([jnp.concatenate(coefs, axis=1), point], axis=0)
        preact = dot3(stack.T, coefs)
        cube = preact * preact
        bend = jnp.tanh(GELU_A * preact * (1.0 + GELU_B * cube))
        half = 0.5 * (1.0 + bend)
        active = preact * half
        slope = half + 0.5 * preact * (1.0 - bend * bend) * (
            GELU_A + (3.0 * GELU_A * GELU_B) * cube
        )
        active = split(active)
        error = mask_ref[pl.ds(x, 1), :] * (dot3(active, proj, NT) - aim)
        rate = dot3(error, proj) * slope
        both = dot3(stack, rate)
        for o in range(4):
            out_ref[pl.ds(512 * o + x, 64, stride=8), :] = both[:64, 128 * o : 128 * o + 128]
        point_grad[...] += both[64:]
        proj_grad[...] += dot3(error.T[:64], active)
        return carry

    lax.fori_loop(0, 8, plane, 0)
    same = iota((64, 512), 0) % 16 == iota((64, 512), 1) % 16
    pick = jnp.where(iota((8, 64), 0) == iota((8, 64), 1) // 16, 1.0, 0.0)
    total = jnp.zeros((8, 128), F32)
    for offset, ref in ((0, point_grad), (32, proj_grad)):
        kept = dot3(pick, jnp.where(same, ref[...], 0.0))
        place = jnp.where(iota((512, 128), 0) // 16 + offset == iota((512, 128), 1), 1.0, 0.0)
        total = total + dot3(kept, place)
    small_ref[...] = total


def reduce_kernel(freq_ref, pieces_ref, out_ref, held_ref):
    lane = iota((256, 128), 1)
    table = wave(rows_waves(freq_ref[0:1, :], lambda part: 32 * ((lane // 32) % 2 - part)))
    table = split(table.T[:64])
    results = [dot3(table, pieces_ref[256 * j : 256 * j + 256, :]) for j in range(8)]
    for part in range(2):
        pieces = regroup([result[32 * part : 32 * part + 32] for result in results])
        for o in range(8):
            held_ref[pl.ds(256 * part + o, 32, stride=8), :] = pieces[o]
    row = iota((256, 128), 0)
    table = wave((row % 128) * freq_ref[1:2, :] + 32 * (lane // 64 - row // 128))
    table = jnp.where(freq_ref[3:4, :] == 1, table, 0.0)
    table = split(table)
    out_ref[...] = dot3(
        jnp.concatenate([held_ref[:256, :], held_ref[256:, :]], axis=1), table
    )


def back_kernel(pieces_ref, modes_ref, lift_ref, weight_ref, small_ref, grad_ref, sum_ref):
    lift = split(lift_ref[...])
    tile = jnp.where(iota((32, 1024), 0) == iota((32, 1024), 1) % 32, SCALE, 0.0).astype(BF16)
    total = jnp.zeros((8, 1024), F32)
    for p in range(4):
        modes = modes_ref[8 * p : 8 * p + 8, :]
        spread = dot3(modes.T, lift)
        grads = jnp.concatenate(
            [pieces_ref[2 * o, p] + pieces_ref[2 * o + 1, p] for o in range(4)], axis=0
        )
        high, low = split(grads.T)
        outer = mul(low, tile, NN) + mul(high, tile, NN)
        real, imag = spread[:64], spread[64:]
        grad_real, grad_imag = outer[:64], outer[64:]
        grad_ref[0, p] = real * grad_real + imag * grad_imag
        grad_ref[1, p] = real * grad_imag - imag * grad_real
        first, second = weight_ref[0, p], weight_ref[1, p]
        back = jnp.concatenate(
            [first * grad_real + second * grad_imag, first * grad_imag - second * grad_real], axis=0
        )
        total = total + dot3(modes, back)
    place = jnp.where(iota((1024, 128), 0) // 32 + 64 == iota((1024, 128), 1), 1.0, 0.0)
    sum_ref[...] = small_ref[...] + dot3(total, place)


def call(kernel, shapes, scratch=(), name=None):
    return pl.pallas_call(
        kernel,
        out_shape=shapes,
        scratch_shapes=list(scratch),
        name=name,
        compiler_params=pltpu.CompilerParams(vmem_limit_bytes=48 * 1024 * 1024),
    )


def array(*shape):
    return jax.ShapeDtypeStruct(shape, F32)


def exchange(value, axes):
    return lax.all_to_all(value, axes, split_axis=0, concat_axis=0, tiled=True)


def spread_rows(matrix):
    padded = jnp.pad(matrix.T, ((0, 1), (0, 0)))
    eye = jnp.eye(16, dtype=F32)
    return (padded[:, None, :, None] * eye[None, :, None, :]).reshape(64, 512)


def body(
    input_field,
    target_field,
    row_mask,
    modes,
    lift_weight,
    mix_weight,
    spectral_weight,
    proj_weight,
):
    parity = lax.axis_index("py") % 2
    first, second, third = modes[0], modes[1], modes[2]
    lanes = jnp.arange(128, dtype=jnp.int32)
    depth = jnp.repeat(third.reshape(16, 2).T.reshape(32), 2)
    outer = jnp.broadcast_to(first.reshape(8, 1, 4), (8, 2, 4)).reshape(64)
    freq = jnp.stack(
        [
            jnp.tile(first, 4),
            jnp.tile(jnp.repeat(second, 2), 2),
            jnp.tile(depth, 2),
            (lanes % 2 == parity).astype(jnp.int32),
            jnp.tile(outer, 2),
            lanes,
            lanes,
            lanes,
        ]
    )
    field = input_field[0]
    target = target_field[0]
    weight = spectral_weight.reshape(2, 4, 64, 1024)
    mask = jnp.tile(2.0 * row_mask.astype(F32), (1, 8))
    lift_rows = jnp.pad(jnp.repeat(lift_weight.T, 32, axis=1), ((0, 5), (0, 0)))
    pointwise = jnp.einsum("cd,dj->cj", mix_weight, lift_weight, precision=lax.Precision.HIGHEST)
    point = spread_rows(pointwise)
    proj = jnp.pad(spread_rows(proj_weight.T), ((0, 64), (0, 0)))

    pieces = call(input_depth, array(256, 128), name="input_depth")(freq, field)
    pieces = exchange(pieces.reshape(16, 16, 128), "px").reshape(256, 128)
    pieces = call(input_rows, array(64, 128), name="input_rows")(freq, pieces)
    pieces = exchange(pieces.reshape(8, 8, 128), "py").reshape(64, 128)
    input_modes, pieces = call(
        mix_kernel,
        (array(32, 128), array(8, 4, 8, 128)),
        [pltpu.VMEM((64, 256), F32)],
        name="mix",
    )(freq, pieces, lift_rows, weight)
    pieces = exchange(pieces, "py").reshape(256, 128)
    pieces = call(expand, array(2048, 128), [pltpu.VMEM((512, 128), F32)], name="expand")(
        freq, pieces
    )
    pieces = exchange(pieces.reshape(128, 16, 128), ("py", "px")).reshape(2048, 128)
    pieces, small = call(
        grid_kernel,
        (array(2048, 128), array(8, 128)),
        [pltpu.VMEM((64, 512), F32), pltpu.VMEM((64, 512), F32)],
        name="grid",
    )(freq, pieces, field, target, mask, point, proj)
    pieces = exchange(pieces.reshape(128, 16, 128), ("py", "px")).reshape(2048, 128)
    pieces = call(reduce_kernel, array(256, 128), [pltpu.VMEM((512, 128), F32)], name="reduce")(
        freq, pieces
    )
    pieces = exchange(pieces.reshape(8, 4, 8, 128), "py")
    grad, sums = call(back_kernel, (array(2, 4, 64, 1024), array(8, 128)), name="back")(
        pieces, input_modes, lift_rows, weight, small
    )
    sums = exchange(jnp.broadcast_to(sums[None, :3], (128, 3, 128)), ("px", "py"))
    sums = jnp.sum(sums, axis=0)
    cross, proj_total, lift_part = sums[:, :32], sums[:, 32:64], sums[:, 64:96]
    high = lax.Precision.HIGHEST
    lift_total = jnp.einsum("dc,jd->cj", mix_weight, cross, precision=high) + lift_part.T
    mix_total = jnp.einsum("jc,dj->cd", cross, lift_weight, precision=high)
    return (
        lift_total * SCALE,
        mix_total * SCALE,
        proj_total * SCALE,
        grad.reshape(spectral_weight.shape),
    )


def solution(mesh):
    in_specs = (
        P(None, None, "px", "py", None),
        P(None, None, "px", "py", None),
        P(("seed", "px"), "py"),
        P("seed", None),
        P("seed", None),
        P("seed", None),
        P("seed", "py", None, "px", None),
        P("seed", None),
    )
    out_specs = (
        P("seed", None),
        P("seed", None),
        P("seed", None),
        P("seed", "py", None, "px", None),
    )
    return jax.shard_map(body, mesh=mesh, in_specs=in_specs, out_specs=out_specs, check_vma=False)
```

```python
import math

import jax
import jax.numpy as jnp
from jax import lax
from jax.experimental import pallas as pl
from jax.experimental.pallas import tpu as pltpu
from jax.sharding import PartitionSpec as P

C = 32
N = 128
M = 32
F32 = jnp.float32
BF16 = jnp.bfloat16
SCALE = 1.0 / float(N**3)
GELU_A = math.sqrt(2.0 / math.pi)
GELU_B = 0.044715

NN = (((1,), (0,)), ((), ()))
NT = (((1,), (1,)), ((), ()))


def split(value):
    high = value.astype(BF16)
    return high, (value - high.astype(F32)).astype(BF16)


def mul(left, right, dims):
    return lax.dot_general(left, right, dims, preferred_element_type=F32)


def dot3(left, right, dims=NN):
    left_high, left_low = left if isinstance(left, tuple) else split(left)
    right_high, right_low = right if isinstance(right, tuple) else split(right)
    return (
        mul(left_low, right_high, dims)
        + mul(left_high, right_low, dims)
        + mul(left_high, right_high, dims)
    )


def iota(shape, axis):
    return lax.broadcasted_iota(jnp.int32, shape, axis)


def wave(turns):
    place = jnp.abs((turns & (N - 1)) - N // 2).astype(F32)
    angle = (place - N / 4) * (2.0 * math.pi / N)
    square = angle * angle
    series = 1.0 / 39916800.0
    for term in (362880.0, 5040.0, 120.0, 6.0, 1.0):
        series = 1.0 / term - square * series
    return angle * series


def dot2k(left, right):
    left_high, left_low = split(left)
    right_high, right_low = right if isinstance(right, tuple) else split(right)
    wide = jnp.concatenate([left_high, left_low], axis=1)
    tall = jnp.concatenate([right_high, right_high], axis=0)
    return mul(left_high, right_low, NN) + mul(wide, tall, NN)


def frequency_rows(modes):
    place = iota((M, 128), 1)
    slot = iota((M, 128), 0)
    modes = modes.astype(F32).astype(BF16)
    orders = (
        (0, place % 32),
        (1, place % 32),
        (2, 2 * (place // 2 % 16) + place // 32 % 2),
        (0, 4 * (place // 8 % 8) + place % 4),
    )
    rows = []
    for dim, order in orders:
        pick = jnp.where(slot == order, 1.0, 0.0).astype(BF16)
        rows.append(mul(modes, pick, NN)[dim : dim + 1])
    return jnp.concatenate(rows + rows, axis=0).astype(jnp.int32)


def regroup(pieces):
    group = iota(pieces[0].shape, 1) // 16
    out = []
    for target in range(8):
        total = pieces[target]
        for source in range(8):
            if source != target:
                moved = pltpu.roll(pieces[source], (16 * (source - target)) % 128, 1)
                total = jnp.where(group == source, moved, total)
        out.append(total)
    return out


def depth_waves(freq):
    shape = (N, 128)
    return wave(iota(shape, 0) * freq + 32 * (iota(shape, 1) & 1))


def input_depth(modes_ref, field_ref, freq_ref, out_ref):
    freq = frequency_rows(modes_ref[...])
    freq_ref[...] = freq
    table = split(depth_waves(freq[2:3]).T[:64])
    lane = iota((32, 128), 1)
    blank = jnp.zeros((16, N), F32)
    for x in range(8):
        rows = [field_ref[channel, x] for channel in range(3)] + [blank]
        both = jnp.concatenate(rows + rows, axis=0)
        result = dot3(table, both, NT)
        out_ref[pl.ds(x, 32, stride=8), :] = jnp.where(lane < 64, result[:32], result[32:])


def rows_waves(freq_row, phase):
    shape = (256, 128)
    row = iota(shape, 0)
    place = (row // 16) * 8 + row % 8
    return place * freq_row + phase(row // 8 % 2)


def input_rows(freq_ref, pieces_ref, out_ref):
    lane = iota((256, 128), 1)
    table = wave(rows_waves(freq_ref[3:4, :], lambda part: 32 * ((lane // 4) % 2 - part)))
    out_ref[...] = dot3(table.T[:64], pieces_ref[...])


def weight_rows(weight_ref, part, p):
    base = 512 * (4 * part + p)
    return jnp.concatenate(
        [
            jnp.concatenate(
                [weight_ref[pl.ds(base + 2 * k + r, 32, stride=16), :] for k in range(8)], axis=1
            )
            for r in range(2)
        ],
        axis=0,
    )


def lift_spread(lift_ref):
    pick = jnp.where(iota((32, 1024), 0) == iota((32, 1024), 1) // 32, 1.0, 0.0).astype(BF16)
    high, low = split(lift_ref[...])
    return mul(low, pick, NN) + mul(high, pick, NN)


def spread_modes(modes, lift):
    turned = modes.T
    total = turned[:, 0:1] * lift[0:1]
    for channel in (1, 2):
        total = total + turned[:, channel : channel + 1] * lift[channel : channel + 1]
    return total


def fold_table():
    return jnp.where(iota((32, 1024), 0) == iota((32, 1024), 1) % 32, SCALE, 0.0).astype(BF16)


def mix_kernel(freq_ref, pieces_ref, lift_ref, weight_ref, held_modes_ref, out_ref, held_ref):
    pieces = [pieces_ref[8 * source : 8 * source + 8, :] for source in range(8)]
    rows = split(jnp.concatenate(regroup(pieces), axis=0))
    shape = (N, 128)
    lane = iota(shape, 1)
    turns = iota(shape, 0) * freq_ref[1:2, :]
    held_ref[:, :128] = dot3(rows, wave(turns + 32 * (lane // 64)))
    held_ref[:, 128:] = dot3(rows, wave(turns + 32 * (lane // 64) - 32))
    first_slot = iota((4, 128), 1) // 32 % 2 == 0
    held_modes_ref[...] = jnp.zeros((32, 128), F32)
    for channel in range(3):
        both = []
        for parity in range(2):
            base = 8 * (4 * parity + channel)
            both.append(held_ref[base : base + 4, :128] + held_ref[base + 4 : base + 8, 128:])
        held_modes_ref[pl.ds(channel, 4, stride=8), :] = jnp.where(first_slot, both[0], both[1])
    lift = lift_spread(lift_ref)
    fold = fold_table()
    for p in range(4):
        spread = spread_modes(held_modes_ref[8 * p : 8 * p + 8, :], lift)
        real, imag = spread[:64], spread[64:]
        first, second = weight_rows(weight_ref, 0, p), weight_rows(weight_ref, 1, p)
        product = jnp.concatenate([first * real - second * imag, second * real + first * imag], axis=0)
        high, low = split(product)
        mixed = mul(fold, low, NT) + mul(fold, high, NT)
        for target in range(8):
            start = 8 * (target // 2)
            out_ref[target, p] = mixed[start : start + 8]


def plane_waves(freq_ref):
    shape = (256, 128)
    row, lane = iota(shape, 0), iota(shape, 1)
    table = wave((row % 128) * freq_ref[1:2, :] + 32 * (lane // 64 - row // 128))
    parity = lax.axis_index("py") % 2
    return split(jnp.where(lane // 32 % 2 == parity, table, 0.0))


def expand(freq_ref, pieces_ref, out_ref, mark_ref, held_ref):
    result = dot3(pieces_ref[...], plane_waves(freq_ref), NT)
    held_ref[:256, :] = result[:, :128]
    held_ref[256:, :] = result[:, 128:]
    parts = []
    for part in range(2):
        parts.append(
            regroup([held_ref[pl.ds(256 * part + o, 32, stride=8), :] for o in range(8)])
        )
    lane = iota((256, 128), 1)
    table = split(wave(rows_waves(freq_ref[0:1, :], lambda part: 32 * (lane // 32 - part)))[:, :64])
    for pair in range(4):
        wide = jnp.concatenate(
            [
                jnp.concatenate([parts[part][2 * pair + k] for part in range(2)], axis=0)
                for k in range(2)
            ],
            axis=1,
        )
        result = dot3(table, wide)
        for k in range(2):
            start = 256 * (2 * pair + k)
            out_ref[start : start + 256, :] = result[:, 128 * k : 128 * k + 128]
    mark_ref[...] = jnp.zeros((8, 128), F32)


def tables_kernel(mark_ref, mask_ref, lift_ref, mix_ref, proj_ref, point_out, proj_out, mask_out):
    pick = jnp.where(iota((32, 512), 0) == iota((32, 512), 1) // 16, 1.0, 0.0).astype(BF16)
    same = iota((64, 512), 0) % 16 == iota((64, 512), 1) % 16
    rows = jnp.where(iota((64, 8), 0) // 16 == iota((64, 8), 1), 1.0, 0.0).astype(BF16)

    def spread(matrix):
        high, low = split(matrix)
        wide = split(mul(high, pick, NN) + mul(low, pick, NN))
        return jnp.where(same, mul(rows, wide[0], NN) + mul(rows, wide[1], NN), 0.0)

    point_out[...] = spread(dot3(lift_ref[...], mix_ref[...], NT))
    table = spread(proj_ref[...])
    proj_out[:64] = table
    proj_out[64:] = table
    repeat = jnp.where(iota((16, 128), 0) == iota((16, 128), 1) % 16, 2.0, 0.0).astype(BF16)
    mask = mul(mask_ref[...].astype(F32).astype(BF16), repeat, NN)
    mask_out[...] = mask + 0.0 * mark_ref[...]


def grid_kernel(
    freq_ref, pieces_ref, field_ref, target_ref, mask_ref, point_ref, proj_ref,
    out_ref, point_grad, proj_grad,
):
    waves = depth_waves(freq_ref[2:3, :]).T[:64]
    point = point_ref[...]
    proj = split(proj_ref[...])
    back = jnp.concatenate(
        [proj[0], proj[1][:64], jnp.zeros((64, 512), BF16)], axis=0
    )
    lower = iota((N, 128), 1) < 64
    blank = jnp.zeros((16, N), F32)
    point_grad[...] = jnp.zeros_like(point_grad)
    proj_grad[...] = jnp.zeros_like(proj_grad)

    def plane(x, carry):
        rows = [field_ref[channel, x] for channel in range(3)] + [blank]
        stack = jnp.concatenate([waves] + rows, axis=0)
        aims = [target_ref[channel, x] for channel in range(3)] + [blank]
        aim = jnp.concatenate(aims + aims, axis=0).T
        coefs = [pieces_ref[pl.ds(512 * o + x, 64, stride=8), :] for o in range(4)]
        coefs = jnp.concatenate([jnp.concatenate(coefs, axis=1), point], axis=0)
        preact = dot2k(stack.T, coefs)
        cube = preact * preact
        bend = jnp.tanh(preact * (GELU_A + (GELU_A * GELU_B) * cube))
        half = 0.5 + 0.5 * bend
        active = split(preact * half)
        slope = half + preact * (0.5 - 0.5 * bend * bend) * (
            GELU_A + (3.0 * GELU_A * GELU_B) * cube
        )
        error = mask_ref[pl.ds(x, 1), :] * (dot3(active, proj, NT) - aim)
        high = error.astype(BF16)
        both = jnp.where(lower, high.astype(F32), error - high.astype(F32)).astype(BF16)
        rate = mul(jnp.concatenate([both, high], axis=1), back, NN) * slope
        both = dot2k(stack, rate)
        for o in range(4):
            out_ref[pl.ds(512 * o + x, 64, stride=8), :] = both[:64, 128 * o : 128 * o + 128]
        point_grad[...] += both[64:]
        proj_grad[...] += dot2k(error.T[:64], active)
        return carry

    lax.fori_loop(0, 8, plane, 0)


def pick_kernel(point_grad, proj_grad, small_ref):
    same = iota((64, 512), 0) % 16 == iota((64, 512), 1) % 16
    pick = jnp.where(iota((8, 64), 0) == iota((8, 64), 1) // 16, 1.0, 0.0)
    total = jnp.zeros((8, 128), F32)
    for offset, ref in ((0, point_grad), (32, proj_grad)):
        kept = dot3(pick, jnp.where(same, ref[...], 0.0))
        place = jnp.where(iota((512, 128), 0) // 16 + offset == iota((512, 128), 1), 1.0, 0.0)
        total = total + dot3(kept, place)
    small_ref[...] = total


def reduce_kernel(freq_ref, pieces_ref, out_ref, held_ref):
    lane = iota((256, 128), 1)
    table = wave(rows_waves(freq_ref[0:1, :], lambda part: 32 * ((lane // 32) % 2 - part)))
    table = split(table.T[:64])
    results = []
    for j in range(8):
        results.append(dot3(table, pieces_ref[256 * j : 256 * j + 256, :]))
    for part in range(2):
        pieces = regroup([result[32 * part : 32 * part + 32] for result in results])
        for o in range(8):
            held_ref[pl.ds(256 * part + o, 32, stride=8), :] = pieces[o]
    rows = jnp.concatenate([held_ref[:256, :], held_ref[256:, :]], axis=1)
    out_ref[...] = dot3(rows, plane_waves(freq_ref))


def outer_grads(pieces_ref, tile, p):
    grads = jnp.concatenate(
        [pieces_ref[2 * o, p] + pieces_ref[2 * o + 1, p] for o in range(4)], axis=0
    )
    return mul(jnp.concatenate(split(grads.T), axis=1), tile, NN)


def lift_kernel(pieces_ref, held_modes_ref, weight_ref, small_ref, sum_ref):
    tile = fold_table()
    tile = jnp.concatenate([tile, tile], axis=0)
    total = [jnp.zeros((1, 1024), F32)] * 3
    for p in range(4):
        outer = outer_grads(pieces_ref, tile, p)
        real, imag = outer[:64], outer[64:]
        first, second = weight_rows(weight_ref, 0, p), weight_rows(weight_ref, 1, p)
        back = jnp.concatenate([first * real + second * imag, first * imag - second * real], axis=0)
        turned = held_modes_ref[8 * p : 8 * p + 8, :].T
        for channel in range(3):
            product = turned[:, channel : channel + 1] * back
            total[channel] = total[channel] + jnp.sum(product, axis=0, keepdims=True)
    total = jnp.concatenate(total + [jnp.zeros((5, 1024), F32)], axis=0)
    place = jnp.where(iota((1024, 128), 0) // 32 + 64 == iota((1024, 128), 1), 1.0, 0.0)
    total = small_ref[...] + dot3(total, place)
    total = jnp.where(iota((8, 128), 0) < 4, total, pltpu.roll(total, 4, 0))
    for target in range(64):
        sum_ref[8 * target : 8 * target + 8, :] = total


def grad_kernel(pieces_ref, held_modes_ref, lift_ref, grad_ref):
    lift = lift_spread(lift_ref)
    tile = fold_table()
    tile = jnp.concatenate([tile, tile], axis=0)
    for p in range(4):
        spread = spread_modes(held_modes_ref[8 * p : 8 * p + 8, :], lift)
        outer = outer_grads(pieces_ref, tile, p)
        real, imag = spread[:64], spread[64:]
        grad_real, grad_imag = outer[:64], outer[64:]
        results = (real * grad_real + imag * grad_imag, real * grad_imag - imag * grad_real)
        for part in range(2):
            base = 512 * (4 * part + p)
            for r in range(2):
                for k in range(8):
                    grad_ref[pl.ds(base + 2 * k + r, 32, stride=16), :] = results[part][
                        32 * r : 32 * r + 32, 128 * k : 128 * k + 128
                    ]


def last_kernel(sum_ref, lift_ref, mix_ref, lift_out, mix_out, proj_out):
    total = jnp.concatenate([sum_ref[...], jnp.zeros((124, 128), F32)], axis=0) * SCALE
    cross = total[:8, :32]
    mix_out[...] = dot3(total.T[:32, :8], lift_ref[...])
    lift_out[...] = (dot3(cross, mix_ref[...]) + total[:8, 64:96])[:3]
    proj_out[...] = total[:3, 32:64]


def call(kernel, shapes, scratch=(), name=None):
    return pl.pallas_call(
        kernel,
        out_shape=shapes,
        scratch_shapes=list(scratch),
        name=name,
        compiler_params=pltpu.CompilerParams(vmem_limit_bytes=48 * 1024 * 1024),
    )


def array(*shape):
    return jax.ShapeDtypeStruct(shape, F32)


def exchange(value, axes):
    return lax.all_to_all(value, axes, split_axis=0, concat_axis=0, tiled=True)


def body(
    input_field,
    target_field,
    row_mask,
    modes,
    lift_weight,
    mix_weight,
    spectral_weight,
    proj_weight,
):
    field = input_field[0]
    target = target_field[0]
    weight = spectral_weight.reshape(2, 4, 32, 2, 8, 128).transpose(0, 1, 2, 4, 3, 5)
    weight = weight.reshape(4096, 128)
    lift_rows = jnp.pad(lift_weight.T, ((0, 5), (0, 0)))
    proj_rows = jnp.pad(proj_weight, ((0, 5), (0, 0)))

    freq, pieces = call(
        input_depth,
        (jax.ShapeDtypeStruct((8, 128), jnp.int32), array(256, 128)),
        name="input_depth",
    )(modes, field)
    pieces = exchange(pieces.reshape(16, 16, 128), "px").reshape(256, 128)
    pieces = call(input_rows, array(64, 128), name="input_rows")(freq, pieces)
    pieces = exchange(pieces.reshape(8, 8, 128), "py").reshape(64, 128)
    held_modes, pieces = call(
        mix_kernel,
        (array(32, 128), array(8, 4, 8, 128)),
        [pltpu.VMEM((64, 256), F32)],
        name="mix",
    )(freq, pieces, lift_rows, weight)
    pieces = exchange(pieces, "py").reshape(256, 128)
    pieces, mark = call(
        expand,
        (array(2048, 128), array(8, 128)),
        [pltpu.VMEM((512, 128), F32)],
        name="expand",
    )(freq, pieces)
    point, proj, mask = call(
        tables_kernel, (array(64, 512), array(128, 512), array(8, 128)), name="tables"
    )(mark, row_mask, lift_rows, mix_weight, proj_rows)
    pieces = exchange(pieces.reshape(128, 16, 128), ("py", "px")).reshape(2048, 128)
    pieces, point_grad, proj_grad = call(
        grid_kernel, (array(2048, 128), array(64, 512), array(64, 512)), name="grid"
    )(freq, pieces, field, target, mask, point, proj)
    small = call(pick_kernel, array(8, 128), name="pick")(point_grad, proj_grad)
    pieces = exchange(pieces.reshape(128, 16, 128), ("py", "px")).reshape(2048, 128)
    pieces = call(reduce_kernel, array(256, 128), [pltpu.VMEM((512, 128), F32)], name="reduce")(
        freq, pieces
    )
    pieces = exchange(pieces.reshape(8, 4, 8, 128), "py")
    sums = call(lift_kernel, array(512, 128), name="lift")(pieces, held_modes, weight, small)
    grad = call(grad_kernel, array(4096, 128), name="grad")(pieces, held_modes, lift_rows)
    sums = exchange(sums.reshape(128, 4, 128), ("px", "py"))
    sums = jnp.sum(sums, axis=0)
    lift_total, mix_total, proj_total = call(
        last_kernel, (array(3, 32), array(32, 32), array(3, 32)), name="last"
    )(sums, lift_rows, mix_weight)
    grad = grad.reshape(2, 4, 32, 8, 2, 128).transpose(0, 1, 2, 4, 3, 5)
    return lift_total.T, mix_total, proj_total, grad.reshape(spectral_weight.shape)


def solution(mesh):
    in_specs = (
        P(None, None, "px", "py", None),
        P(None, None, "px", "py", None),
        P(("seed", "px"), "py"),
        P("seed", None),
        P("seed", None),
        P("seed", None),
        P("seed", "py", None, "px", None),
        P("seed", None),
    )
    out_specs = (
        P("seed", None),
        P("seed", None),
        P("seed", None),
        P("seed", "py", None, "px", None),
    )
    return jax.shard_map(body, mesh=mesh, in_specs=in_specs, out_specs=out_specs, check_vma=False)
```

```python
import math

import jax
import jax.numpy as jnp
from jax import lax
from jax.experimental import pallas as pl
from jax.experimental.pallas import tpu as pltpu
from jax.sharding import PartitionSpec as P

C = 32
N = 128
M = 32
F32 = jnp.float32
BF16 = jnp.bfloat16
SCALE = 1.0 / float(N**3)
GELU_A = math.sqrt(2.0 / math.pi)
GELU_B = 0.044715

NN = (((1,), (0,)), ((), ()))
NT = (((1,), (1,)), ((), ()))


def split(value):
    high = value.astype(BF16)
    return high, (value - high.astype(F32)).astype(BF16)


def mul(left, right, dims):
    return lax.dot_general(left, right, dims, preferred_element_type=F32)


def dot3(left, right, dims=NN):
    left_high, left_low = left if isinstance(left, tuple) else split(left)
    right_high, right_low = right if isinstance(right, tuple) else split(right)
    return (
        mul(left_low, right_high, dims)
        + mul(left_high, right_low, dims)
        + mul(left_high, right_high, dims)
    )


def iota(shape, axis):
    return lax.broadcasted_iota(jnp.int32, shape, axis)


def wave(turns):
    place = jnp.abs((turns & (N - 1)) - N // 2).astype(F32)
    angle = (place - N / 4) * (2.0 * math.pi / N)
    square = angle * angle
    series = 1.0 / 39916800.0
    for term in (362880.0, 5040.0, 120.0, 6.0, 1.0):
        series = 1.0 / term - square * series
    return angle * series


def dot2k(left, right):
    left_high, left_low = split(left)
    right_high, right_low = right if isinstance(right, tuple) else split(right)
    wide = jnp.concatenate([left_high, left_low], axis=1)
    tall = jnp.concatenate([right_high, right_high], axis=0)
    return mul(left_high, right_low, NN) + mul(wide, tall, NN)


def frequency_rows(modes):
    place = iota((M, 128), 1)
    slot = iota((M, 128), 0)
    modes = modes.astype(F32).astype(BF16)
    orders = (
        (0, place % 32),
        (1, place % 32),
        (2, 2 * (place // 2 % 16) + place // 32 % 2),
        (0, 4 * (place // 8 % 8) + place % 4),
    )
    rows = []
    for dim, order in orders:
        pick = jnp.where(slot == order, 1.0, 0.0).astype(BF16)
        rows.append(mul(modes, pick, NN)[dim : dim + 1])
    return jnp.concatenate(rows + rows, axis=0).astype(jnp.int32)


def regroup(pieces):
    group = iota(pieces[0].shape, 1) // 16
    out = []
    for target in range(8):
        total = pieces[target]
        for source in range(8):
            if source != target:
                moved = pltpu.roll(pieces[source], (16 * (source - target)) % 128, 1)
                total = jnp.where(group == source, moved, total)
        out.append(total)
    return out


def depth_waves(freq):
    shape = (N, 128)
    return wave(iota(shape, 0) * freq + 32 * (iota(shape, 1) & 1))


def input_depth(modes_ref, field_ref, freq_ref, out_ref):
    freq = frequency_rows(modes_ref[...])
    freq_ref[...] = freq
    table = split(depth_waves(freq[2:3]).T[:64])
    lane = iota((32, 128), 1)
    blank = jnp.zeros((16, N), F32)
    for x in range(8):
        rows = [field_ref[channel, x] for channel in range(3)] + [blank]
        both = jnp.concatenate(rows + rows, axis=0)
        result = dot3(table, both, NT)
        out_ref[pl.ds(x, 32, stride=8), :] = jnp.where(lane < 64, result[:32], result[32:])


def rows_waves(freq_row, phase):
    shape = (256, 128)
    row = iota(shape, 0)
    place = (row // 16) * 8 + row % 8
    return place * freq_row + phase(row // 8 % 2)


def input_rows(freq_ref, pieces_ref, out_ref):
    lane = iota((256, 128), 1)
    table = wave(rows_waves(freq_ref[3:4, :], lambda part: 32 * ((lane // 4) % 2 - part)))
    out_ref[...] = dot3(table.T[:64], pieces_ref[...])


def weight_rows(weight_ref, part, p):
    base = 512 * (4 * part + p)
    return jnp.concatenate(
        [
            jnp.concatenate(
                [weight_ref[pl.ds(base + 2 * k + r, 32, stride=16), :] for k in range(8)], axis=1
            )
            for r in range(2)
        ],
        axis=0,
    )


def lift_spread(lift_ref):
    pick = jnp.where(iota((32, 1024), 0) == iota((32, 1024), 1) // 32, 1.0, 0.0).astype(BF16)
    high, low = split(lift_ref[...])
    return mul(low, pick, NN) + mul(high, pick, NN)


def spread_modes(modes, lift):
    turned = modes.T
    total = turned[:, 0:1] * lift[0:1]
    for channel in (1, 2):
        total = total + turned[:, channel : channel + 1] * lift[channel : channel + 1]
    return total


def fold_table():
    return jnp.where(iota((32, 1024), 0) == iota((32, 1024), 1) % 32, SCALE, 0.0).astype(BF16)


def input_planes(freq_ref, pieces_ref, held_modes_ref, held_ref):
    pieces = [pieces_ref[8 * source : 8 * source + 8, :] for source in range(8)]
    rows = split(jnp.concatenate(regroup(pieces), axis=0))
    shape = (N, 128)
    lane = iota(shape, 1)
    turns = iota(shape, 0) * freq_ref[1:2, :]
    held_ref[:, :128] = dot3(rows, wave(turns + 32 * (lane // 64)))
    held_ref[:, 128:] = dot3(rows, wave(turns + 32 * (lane // 64) - 32))
    first_slot = iota((4, 128), 1) // 32 % 2 == 0
    held_modes_ref[...] = jnp.zeros((32, 128), F32)
    for channel in range(3):
        both = []
        for parity in range(2):
            base = 8 * (4 * parity + channel)
            both.append(held_ref[base : base + 4, :128] + held_ref[base + 4 : base + 8, 128:])
        held_modes_ref[pl.ds(channel, 4, stride=8), :] = jnp.where(first_slot, both[0], both[1])


def mix_kernel(held_modes_ref, lift_ref, weight_ref, out_ref):
    lift = lift_spread(lift_ref)
    fold = fold_table()
    for p in range(4):
        spread = spread_modes(held_modes_ref[8 * p : 8 * p + 8, :], lift)
        real, imag = spread[:64], spread[64:]
        first, second = weight_rows(weight_ref, 0, p), weight_rows(weight_ref, 1, p)
        product = jnp.concatenate([first * real - second * imag, second * real + first * imag], axis=0)
        high, low = split(product)
        mixed = mul(fold, low, NT) + mul(fold, high, NT)
        for target in range(8):
            start = 8 * (target // 2)
            out_ref[target, p] = mixed[start : start + 8]


def plane_waves(freq_ref, slot_ref):
    shape = (256, 128)
    row, lane = iota(shape, 0), iota(shape, 1)
    table = wave((row % 128) * freq_ref[1:2, :] + 32 * (lane // 64 - row // 128))
    return split(jnp.where(slot_ref[...] == 1, table, 0.0))


def expand(freq_ref, slot_ref, pieces_ref, out_hbm, mark_ref, held_ref, out_ref, sems):
    result = dot3(pieces_ref[...], plane_waves(freq_ref, slot_ref), NT)
    held_ref[:256, :] = result[:, :128]
    held_ref[256:, :] = result[:, 128:]
    parts = []
    for part in range(2):
        parts.append(
            regroup([held_ref[pl.ds(256 * part + o, 32, stride=8), :] for o in range(8)])
        )
    lane = iota((256, 128), 1)
    table = split(wave(rows_waves(freq_ref[0:1, :], lambda part: 32 * (lane // 32 - part)))[:, :64])
    copies = []
    for pair in range(4):
        wide = jnp.concatenate(
            [
                jnp.concatenate([parts[part][2 * pair + k] for part in range(2)], axis=0)
                for k in range(2)
            ],
            axis=1,
        )
        result = dot3(table, wide)
        for k in range(2):
            start = 256 * (2 * pair + k)
            out_ref[start : start + 256, :] = result[:, 128 * k : 128 * k + 128]
        rows = pl.ds(512 * pair, 512)
        copies.append(
            pltpu.make_async_copy(out_ref.at[rows, :], out_hbm.at[rows, :], sems.at[pair])
        )
        copies[pair].start()
    mark_ref[...] = jnp.zeros((8, 128), F32)
    for copy in copies:
        copy.wait()


def tables_kernel(mark_ref, mask_ref, lift_ref, mix_ref, proj_ref, point_out, proj_out, mask_out):
    pick = jnp.where(iota((32, 512), 0) == iota((32, 512), 1) // 16, 1.0, 0.0).astype(BF16)
    same = iota((64, 512), 0) % 16 == iota((64, 512), 1) % 16
    rows = jnp.where(iota((64, 8), 0) // 16 == iota((64, 8), 1), 1.0, 0.0).astype(BF16)

    def spread(matrix):
        high, low = split(matrix)
        wide = split(mul(high, pick, NN) + mul(low, pick, NN))
        return jnp.where(same, mul(rows, wide[0], NN) + mul(rows, wide[1], NN), 0.0)

    point_out[...] = spread(dot3(lift_ref[...], mix_ref[...], NT))
    table = spread(proj_ref[...])
    proj_out[:64] = table
    proj_out[64:] = table
    repeat = jnp.where(iota((16, 128), 0) == iota((16, 128), 1) % 16, 2.0, 0.0).astype(BF16)
    mask = mul(mask_ref[...].astype(F32).astype(BF16), repeat, NN)
    mask_out[...] = mask + 0.0 * mark_ref[...]


def grid_kernel(
    freq_ref, pieces_ref, field_ref, target_ref, mask_ref, point_ref, proj_ref,
    out_ref, point_grad, proj_grad,
):
    waves = depth_waves(freq_ref[2:3, :]).T[:64]
    point = point_ref[...]
    proj = split(proj_ref[...])
    back = jnp.concatenate(
        [proj[0], proj[1][:64], jnp.zeros((64, 512), BF16)], axis=0
    )
    lower = iota((N, 128), 1) < 64
    blank = jnp.zeros((16, N), F32)
    point_grad[...] = jnp.zeros_like(point_grad)
    proj_grad[...] = jnp.zeros_like(proj_grad)

    def plane(x, carry):
        rows = [field_ref[channel, x] for channel in range(3)] + [blank]
        stack = jnp.concatenate([waves] + rows, axis=0)
        aims = [target_ref[channel, x] for channel in range(3)] + [blank]
        aim = jnp.concatenate(aims + aims, axis=0).T
        coefs = [pieces_ref[pl.ds(512 * o + x, 64, stride=8), :] for o in range(4)]
        coefs = jnp.concatenate([jnp.concatenate(coefs, axis=1), point], axis=0)
        preact = dot2k(stack.T, coefs)
        cube = preact * preact
        bend = jnp.tanh(preact * (GELU_A + (GELU_A * GELU_B) * cube))
        half = 0.5 + 0.5 * bend
        active = split(preact * half)
        slope = half + preact * (0.5 - 0.5 * bend * bend) * (
            GELU_A + (3.0 * GELU_A * GELU_B) * cube
        )
        error = mask_ref[pl.ds(x, 1), :] * (dot3(active, proj, NT) - aim)
        high = error.astype(BF16)
        both = jnp.where(lower, high.astype(F32), error - high.astype(F32)).astype(BF16)
        rate = mul(jnp.concatenate([both, high], axis=1), back, NN) * slope
        both = dot2k(stack, rate)
        for o in range(4):
            out_ref[pl.ds(512 * o + x, 64, stride=8), :] = both[:64, 128 * o : 128 * o + 128]
        point_grad[...] += both[64:]
        proj_grad[...] += dot2k(error.T[:64], active)
        return carry

    lax.fori_loop(0, 8, plane, 0, unroll=8)


def pick_kernel(point_grad, proj_grad, small_ref):
    same = iota((64, 512), 0) % 16 == iota((64, 512), 1) % 16
    pick = jnp.where(iota((8, 64), 0) == iota((8, 64), 1) // 16, 1.0, 0.0)
    total = jnp.zeros((8, 128), F32)
    for offset, ref in ((0, point_grad), (32, proj_grad)):
        kept = dot3(pick, jnp.where(same, ref[...], 0.0))
        place = jnp.where(iota((512, 128), 0) // 16 + offset == iota((512, 128), 1), 1.0, 0.0)
        total = total + dot3(kept, place)
    small_ref[...] = total


def reduce_kernel(freq_ref, slot_ref, pieces_ref, out_ref, held_ref):
    lane = iota((256, 128), 1)
    table = wave(rows_waves(freq_ref[0:1, :], lambda part: 32 * ((lane // 32) % 2 - part)))
    table = split(table.T[:64])
    results = []
    for j in range(8):
        results.append(dot3(table, pieces_ref[256 * j : 256 * j + 256, :]))
    for part in range(2):
        pieces = regroup([result[32 * part : 32 * part + 32] for result in results])
        for o in range(8):
            held_ref[pl.ds(256 * part + o, 32, stride=8), :] = pieces[o]
    rows = jnp.concatenate([held_ref[:256, :], held_ref[256:, :]], axis=1)
    out_ref[...] = dot3(rows, plane_waves(freq_ref, slot_ref))


def outer_grads(pieces_ref, tile, p):
    grads = jnp.concatenate(
        [pieces_ref[2 * o, p] + pieces_ref[2 * o + 1, p] for o in range(4)], axis=0
    )
    return mul(jnp.concatenate(split(grads.T), axis=1), tile, NN)


def lift_kernel(pieces_ref, held_modes_ref, weight_ref, small_ref, sum_ref):
    tile = jnp.where(iota((32, 128), 0) == iota((32, 128), 1) % 32, SCALE, 0.0).astype(BF16)
    tile = jnp.concatenate([tile, tile], axis=0)
    even = iota((8, 128), 0) % 2 == 0
    total = [[jnp.zeros((8, 128), F32)] * 2 for channel in range(3)]
    for p in range(4):
        outer = outer_grads(pieces_ref, tile, p)
        real, imag = outer[:64], outer[64:]
        turned = held_modes_ref[8 * p : 8 * p + 8, :].T
        pairs = []
        for channel in range(3):
            first = turned[:64, channel : channel + 1]
            second = turned[64:, channel : channel + 1]
            pairs.append((first * real + second * imag, first * imag - second * real))
        for q in range(32):
            rows = [
                [weight_ref[pl.ds(512 * (4 * part + p) + 16 * q + 8 * k, 8), :] for k in range(2)]
                for part in range(2)
            ]
            for channel in range(3):
                for part in range(2):
                    pair = pairs[channel][part]
                    both = jnp.where(even, pair[q : q + 1], pair[32 + q : 33 + q])
                    for k in range(2):
                        total[channel][k] = total[channel][k] + both * rows[part][k]
    lane = iota((128, 128), 1)
    gather = jnp.where((lane >= 64) & (lane < 96) & (lane % 4 == iota((128, 128), 0) // 32), 1.0, 0.0)
    owner = (iota((16, 128), 1) - 64) // 4 == iota((16, 128), 0) // 2
    lines = []
    for channel in range(3):
        lines.append(
            jnp.sum(
                jnp.where(owner, dot3(jnp.concatenate(total[channel], axis=0), gather), 0.0),
                axis=0,
                keepdims=True,
            )
        )
    total = small_ref[...] + jnp.concatenate(lines + [jnp.zeros((5, 128), F32)], axis=0)
    total = jnp.where(iota((8, 128), 0) < 4, total, pltpu.roll(total, 4, 0))
    for target in range(64):
        sum_ref[8 * target : 8 * target + 8, :] = total


def grad_kernel(pieces_ref, held_modes_ref, lift_ref, grad_ref):
    lift = lift_spread(lift_ref)
    tile = fold_table()
    tile = jnp.concatenate([tile, tile], axis=0)
    for p in range(4):
        spread = spread_modes(held_modes_ref[8 * p : 8 * p + 8, :], lift)
        outer = outer_grads(pieces_ref, tile, p)
        real, imag = spread[:64], spread[64:]
        grad_real, grad_imag = outer[:64], outer[64:]
        results = (real * grad_real + imag * grad_imag, real * grad_imag - imag * grad_real)
        for part in range(2):
            base = 512 * (4 * part + p)
            for r in range(2):
                for k in range(8):
                    grad_ref[pl.ds(base + 2 * k + r, 32, stride=16), :] = results[part][
                        32 * r : 32 * r + 32, 128 * k : 128 * k + 128
                    ]


def last_kernel(sum_ref, lift_ref, mix_ref, lift_out, mix_out, proj_out):
    total = jnp.concatenate([sum_ref[...], jnp.zeros((124, 128), F32)], axis=0) * SCALE
    cross = total[:8, :32]
    mix_out[...] = dot3(total.T[:32, :8], lift_ref[...])
    lift_out[...] = (dot3(cross, mix_ref[...]) + total[:8, 64:96])[:3]
    proj_out[...] = total[:3, 32:64]


def call(kernel, shapes, scratch=(), places=None, name=None):
    specs = {}
    if places is not None:
        specs["out_specs"] = tuple(pl.BlockSpec(memory_space=place) for place in places)
    return pl.pallas_call(
        kernel,
        out_shape=shapes,
        scratch_shapes=list(scratch),
        name=name,
        compiler_params=pltpu.CompilerParams(vmem_limit_bytes=48 * 1024 * 1024),
        **specs,
    )


def array(*shape):
    return jax.ShapeDtypeStruct(shape, F32)


def exchange(value, axes):
    return lax.all_to_all(value, axes, split_axis=0, concat_axis=0, tiled=True)


def body(
    input_field,
    target_field,
    row_mask,
    modes,
    lift_weight,
    mix_weight,
    spectral_weight,
    proj_weight,
):
    slot = jnp.arange(128, dtype=jnp.int32) // 32 % 2 == lax.axis_index("py") % 2
    slot = slot.astype(jnp.int32)[None]
    field = input_field[0]
    target = target_field[0]
    weight = spectral_weight.reshape(2, 4, 32, 2, 8, 128).transpose(0, 1, 2, 4, 3, 5)
    weight = weight.reshape(4096, 128)
    lift_rows = jnp.pad(lift_weight.T, ((0, 5), (0, 0)))
    proj_rows = jnp.pad(proj_weight, ((0, 5), (0, 0)))

    freq, pieces = call(
        input_depth,
        (jax.ShapeDtypeStruct((8, 128), jnp.int32), array(256, 128)),
        name="input_depth",
    )(modes, field)
    pieces = exchange(pieces.reshape(16, 16, 128), "px").reshape(256, 128)
    pieces = call(input_rows, array(64, 128), name="input_rows")(freq, pieces)
    pieces = exchange(pieces.reshape(8, 8, 128), "py").reshape(64, 128)
    held_modes = call(
        input_planes, array(32, 128), [pltpu.VMEM((64, 256), F32)], name="input_planes"
    )(freq, pieces)
    pieces = call(mix_kernel, array(8, 4, 8, 128), name="mix")(held_modes, lift_rows, weight)
    pieces = exchange(pieces, "py").reshape(256, 128)
    pieces, mark = call(
        expand,
        (array(2048, 128), array(8, 128)),
        [
            pltpu.VMEM((512, 128), F32),
            pltpu.VMEM((2048, 128), F32),
            pltpu.SemaphoreType.DMA((4,)),
        ],
        (pltpu.HBM, pltpu.VMEM),
        name="expand",
    )(freq, slot, pieces)
    point, proj, mask = call(
        tables_kernel, (array(64, 512), array(128, 512), array(8, 128)), name="tables"
    )(mark, row_mask, lift_rows, mix_weight, proj_rows)
    pieces = exchange(pieces.reshape(128, 16, 128), ("py", "px")).reshape(2048, 128)
    pieces, point_grad, proj_grad = call(
        grid_kernel, (array(2048, 128), array(64, 512), array(64, 512)), name="grid"
    )(freq, pieces, field, target, mask, point, proj)
    small = call(pick_kernel, array(8, 128), name="pick")(point_grad, proj_grad)
    pieces = exchange(pieces.reshape(128, 16, 128), ("py", "px")).reshape(2048, 128)
    pieces = call(reduce_kernel, array(256, 128), [pltpu.VMEM((512, 128), F32)], name="reduce")(
        freq, slot, pieces
    )
    pieces = exchange(pieces.reshape(8, 4, 8, 128), "py")
    sums = call(lift_kernel, array(512, 128), name="lift")(pieces, held_modes, weight, small)
    grad = call(grad_kernel, array(4096, 128), name="grad")(pieces, held_modes, lift_rows)
    sums = exchange(sums.reshape(128, 4, 128), ("px", "py"))
    sums = jnp.sum(sums, axis=0)
    lift_total, mix_total, proj_total = call(
        last_kernel, (array(3, 32), array(32, 32), array(3, 32)), name="last"
    )(sums, lift_rows, mix_weight)
    grad = grad.reshape(2, 4, 32, 8, 2, 128).transpose(0, 1, 2, 4, 3, 5)
    return lift_total.T, mix_total, proj_total, grad.reshape(spectral_weight.shape)


def solution(mesh):
    in_specs = (
        P(None, None, "px", "py", None),
        P(None, None, "px", "py", None),
        P(("seed", "px"), "py"),
        P("seed", None),
        P("seed", None),
        P("seed", None),
        P("seed", "py", None, "px", None),
        P("seed", None),
    )
    out_specs = (
        P("seed", None),
        P("seed", None),
        P("seed", None),
        P("seed", "py", None, "px", None),
    )
    return jax.shard_map(body, mesh=mesh, in_specs=in_specs, out_specs=out_specs, check_vma=False)
```

```python
import math

import jax
import jax.numpy as jnp
from jax import lax
from jax.experimental import pallas as pl
from jax.experimental.pallas import tpu as pltpu
from jax.sharding import PartitionSpec as P

C = 32
N = 128
M = 32
F32 = jnp.float32
BF16 = jnp.bfloat16
SCALE = 1.0 / float(N**3)
GELU_A = math.sqrt(2.0 / math.pi)
GELU_B = 0.044715

NN = (((1,), (0,)), ((), ()))
NT = (((1,), (1,)), ((), ()))


def split(value):
    high = value.astype(BF16)
    return high, (value - high.astype(F32)).astype(BF16)


def mul(left, right, dims):
    return lax.dot_general(left, right, dims, preferred_element_type=F32)


def dot3(left, right, dims=NN):
    left_high, left_low = left if isinstance(left, tuple) else split(left)
    right_high, right_low = right if isinstance(right, tuple) else split(right)
    return (
        mul(left_low, right_high, dims)
        + mul(left_high, right_low, dims)
        + mul(left_high, right_high, dims)
    )


def iota(shape, axis):
    return lax.broadcasted_iota(jnp.int32, shape, axis)


def wave(turns):
    place = jnp.abs((turns & (N - 1)) - N // 2).astype(F32)
    angle = (place - N / 4) * (2.0 * math.pi / N)
    square = angle * angle
    series = 1.0 / 39916800.0
    for term in (362880.0, 5040.0, 120.0, 6.0, 1.0):
        series = 1.0 / term - square * series
    return angle * series


def dot2k(left, right):
    left_high, left_low = split(left)
    right_high, right_low = right if isinstance(right, tuple) else split(right)
    wide = jnp.concatenate([left_high, left_low], axis=1)
    tall = jnp.concatenate([right_high, right_high], axis=0)
    return mul(left_high, right_low, NN) + mul(wide, tall, NN)


def frequency_rows(modes):
    place = iota((M, 128), 1)
    slot = iota((M, 128), 0)
    modes = modes.astype(F32).astype(BF16)
    orders = (
        (0, place % 32),
        (1, place % 32),
        (2, 2 * (place // 2 % 16) + place // 32 % 2),
        (0, 4 * (place // 8 % 8) + place % 4),
    )
    rows = []
    for dim, order in orders:
        pick = jnp.where(slot == order, 1.0, 0.0).astype(BF16)
        rows.append(mul(modes, pick, NN)[dim : dim + 1])
    return jnp.concatenate(rows + rows, axis=0).astype(jnp.int32)


def regroup(pieces):
    group = iota(pieces[0].shape, 1) // 16
    out = []
    for target in range(8):
        total = pieces[target]
        for source in range(8):
            if source != target:
                moved = pltpu.roll(pieces[source], (16 * (source - target)) % 128, 1)
                total = jnp.where(group == source, moved, total)
        out.append(total)
    return out


def depth_waves(freq):
    shape = (N, 128)
    return wave(iota(shape, 0) * freq + 32 * (iota(shape, 1) & 1))


def input_depth(modes_ref, field_ref, freq_ref, out_ref):
    freq = frequency_rows(modes_ref[...])
    freq_ref[...] = freq
    table = split(depth_waves(freq[2:3]).T[:64])
    lane = iota((32, 128), 1)
    blank = jnp.zeros((16, N), F32)
    for x in range(8):
        rows = [field_ref[channel, x] for channel in range(3)] + [blank]
        both = jnp.concatenate(rows + rows, axis=0)
        result = dot3(table, both, NT)
        out_ref[pl.ds(x, 32, stride=8), :] = jnp.where(lane < 64, result[:32], result[32:])


def rows_waves(freq_row, phase):
    shape = (256, 128)
    row = iota(shape, 0)
    place = (row // 16) * 8 + row % 8
    return place * freq_row + phase(row // 8 % 2)


def input_rows(freq_ref, pieces_ref, out_ref):
    lane = iota((256, 128), 1)
    table = wave(rows_waves(freq_ref[3:4, :], lambda part: 32 * ((lane // 4) % 2 - part)))
    out_ref[...] = dot3(table.T[:64], pieces_ref[...])


def weight_rows(weight_ref, part, p):
    base = 512 * (4 * part + p)
    return jnp.concatenate(
        [
            jnp.concatenate(
                [weight_ref[pl.ds(base + 2 * k + r, 32, stride=16), :] for k in range(8)], axis=1
            )
            for r in range(2)
        ],
        axis=0,
    )


def lift_spread(lift_ref):
    pick = jnp.where(iota((32, 1024), 0) == iota((32, 1024), 1) // 32, 1.0, 0.0).astype(BF16)
    high, low = split(lift_ref[...])
    return mul(low, pick, NN) + mul(high, pick, NN)


def spread_modes(modes, lift):
    turned = modes.T
    total = turned[:, 0:1] * lift[0:1]
    for channel in (1, 2):
        total = total + turned[:, channel : channel + 1] * lift[channel : channel + 1]
    return total


def fold_table():
    return jnp.where(iota((32, 1024), 0) == iota((32, 1024), 1) % 32, SCALE, 0.0).astype(BF16)


def mix_kernel(freq_ref, pieces_ref, lift_ref, weight_ref, held_modes_ref, out_ref, held_ref):
    pieces = [pieces_ref[8 * source : 8 * source + 8, :] for source in range(8)]
    rows = split(jnp.concatenate(regroup(pieces), axis=0))
    shape = (N, 128)
    lane = iota(shape, 1)
    turns = iota(shape, 0) * freq_ref[1:2, :]
    held_ref[:, :128] = dot3(rows, wave(turns + 32 * (lane // 64)))
    held_ref[:, 128:] = dot3(rows, wave(turns + 32 * (lane // 64) - 32))
    first_slot = iota((4, 128), 1) // 32 % 2 == 0
    held_modes_ref[...] = jnp.zeros((32, 128), F32)
    for channel in range(3):
        both = []
        for parity in range(2):
            base = 8 * (4 * parity + channel)
            both.append(held_ref[base : base + 4, :128] + held_ref[base + 4 : base + 8, 128:])
        held_modes_ref[pl.ds(channel, 4, stride=8), :] = jnp.where(first_slot, both[0], both[1])
    lift = lift_spread(lift_ref)
    fold = fold_table()
    for p in range(4):
        spread = spread_modes(held_modes_ref[8 * p : 8 * p + 8, :], lift)
        real, imag = spread[:64], spread[64:]
        first, second = weight_rows(weight_ref, 0, p), weight_rows(weight_ref, 1, p)
        product = jnp.concatenate([first * real - second * imag, second * real + first * imag], axis=0)
        high, low = split(product)
        mixed = mul(fold, low, NT) + mul(fold, high, NT)
        for target in range(8):
            start = 8 * (target // 2)
            out_ref[target, p] = mixed[start : start + 8]


def plane_waves(freq_ref):
    shape = (256, 128)
    row, lane = iota(shape, 0), iota(shape, 1)
    table = wave((row % 128) * freq_ref[1:2, :] + 32 * (lane // 64 - row // 128))
    parity = lax.axis_index("py") % 2
    return split(jnp.where(lane // 32 % 2 == parity, table, 0.0))


def expand(freq_ref, pieces_ref, out_hbm, mark_ref, held_ref, out_ref, sems):
    result = dot3(pieces_ref[...], plane_waves(freq_ref), NT)
    held_ref[:256, :] = result[:, :128]
    held_ref[256:, :] = result[:, 128:]
    parts = []
    for part in range(2):
        parts.append(
            regroup([held_ref[pl.ds(256 * part + o, 32, stride=8), :] for o in range(8)])
        )
    lane = iota((256, 128), 1)
    table = split(wave(rows_waves(freq_ref[0:1, :], lambda part: 32 * (lane // 32 - part)))[:, :64])
    copies = []
    for pair in range(4):
        wide = jnp.concatenate(
            [
                jnp.concatenate([parts[part][2 * pair + k] for part in range(2)], axis=0)
                for k in range(2)
            ],
            axis=1,
        )
        result = dot3(table, wide)
        for k in range(2):
            start = 256 * (2 * pair + k)
            out_ref[start : start + 256, :] = result[:, 128 * k : 128 * k + 128]
        rows = pl.ds(512 * pair, 512)
        copies.append(
            pltpu.make_async_copy(out_ref.at[rows, :], out_hbm.at[rows, :], sems.at[pair])
        )
        copies[pair].start()
    mark_ref[...] = jnp.zeros((8, 128), F32)
    for copy in copies:
        copy.wait()


def tables_kernel(mark_ref, mask_ref, lift_ref, mix_ref, proj_ref, point_out, proj_out, mask_out):
    pick = jnp.where(iota((32, 512), 0) == iota((32, 512), 1) // 16, 1.0, 0.0).astype(BF16)
    same = iota((64, 512), 0) % 16 == iota((64, 512), 1) % 16
    owner = iota((64, 512), 0) // 16

    def spread(matrix):
        high, low = split(matrix)
        wide = mul(high, pick, NN) + mul(low, pick, NN)
        total = jnp.zeros((64, 512), F32)
        for channel in range(3):
            total = jnp.where(same & (owner == channel), wide[channel : channel + 1], total)
        return total

    point_out[...] = spread(dot3(lift_ref[...], mix_ref[...], NT))
    table = spread(proj_ref[...])
    proj_out[:64] = table
    proj_out[64:] = table
    repeat = jnp.where(iota((16, 128), 0) == iota((16, 128), 1) % 16, 2.0, 0.0).astype(BF16)
    mask = mul(mask_ref[...].astype(F32).astype(BF16), repeat, NN)
    mask_out[...] = mask + 0.0 * mark_ref[...]


def grid_kernel(
    freq_ref, pieces_ref, field_ref, target_ref, mask_ref, point_ref, proj_ref,
    out_ref, point_grad, proj_grad,
):
    waves = depth_waves(freq_ref[2:3, :]).T[:64]
    point = point_ref[...]
    proj = split(proj_ref[...])
    back = jnp.concatenate(
        [proj[0], proj[1][:64], jnp.zeros((64, 512), BF16)], axis=0
    )
    lower = iota((N, 128), 1) < 64
    blank = jnp.zeros((16, N), F32)
    point_grad[...] = jnp.zeros_like(point_grad)
    proj_grad[...] = jnp.zeros_like(proj_grad)

    def plane(x, carry):
        rows = [field_ref[channel, x] for channel in range(3)] + [blank]
        stack = jnp.concatenate([waves] + rows, axis=0)
        aims = [target_ref[channel, x] for channel in range(3)] + [blank]
        aim = jnp.concatenate(aims + aims, axis=0).T
        coefs = [pieces_ref[pl.ds(512 * o + x, 64, stride=8), :] for o in range(4)]
        coefs = jnp.concatenate([jnp.concatenate(coefs, axis=1), point], axis=0)
        preact = dot2k(stack.T, coefs)
        cube = preact * preact
        bend = jnp.tanh(preact * (GELU_A + (GELU_A * GELU_B) * cube))
        half = 0.5 + 0.5 * bend
        active = split(preact * half)
        slope = half + preact * (0.5 - 0.5 * bend * bend) * (
            GELU_A + (3.0 * GELU_A * GELU_B) * cube
        )
        error = mask_ref[pl.ds(x, 1), :] * (dot3(active, proj, NT) - aim)
        high = error.astype(BF16)
        both = jnp.where(lower, high.astype(F32), error - high.astype(F32)).astype(BF16)
        rate = mul(jnp.concatenate([both, high], axis=1), back, NN) * slope
        both = dot2k(stack, rate)
        for o in range(4):
            out_ref[pl.ds(512 * o + x, 64, stride=8), :] = both[:64, 128 * o : 128 * o + 128]
        point_grad[...] += both[64:]
        proj_grad[...] += dot2k(error.T[:64], active)
        return carry

    lax.fori_loop(0, 8, plane, 0, unroll=8)


def pick_kernel(point_grad, proj_grad, small_ref):
    same = iota((64, 512), 0) % 16 == iota((64, 512), 1) % 16
    pick = jnp.where(iota((8, 64), 0) == iota((8, 64), 1) // 16, 1.0, 0.0)
    total = jnp.zeros((8, 128), F32)
    for offset, ref in ((0, point_grad), (32, proj_grad)):
        kept = dot3(pick, jnp.where(same, ref[...], 0.0))
        place = jnp.where(iota((512, 128), 0) // 16 + offset == iota((512, 128), 1), 1.0, 0.0)
        total = total + dot3(kept, place)
    small_ref[...] = total


def reduce_kernel(freq_ref, pieces_ref, out_ref, held_ref):
    lane = iota((256, 128), 1)
    table = wave(rows_waves(freq_ref[0:1, :], lambda part: 32 * ((lane // 32) % 2 - part)))
    table = split(table.T[:64])
    results = []
    for j in range(8):
        results.append(dot3(table, pieces_ref[256 * j : 256 * j + 256, :]))
    for part in range(2):
        pieces = regroup([result[32 * part : 32 * part + 32] for result in results])
        for o in range(8):
            held_ref[pl.ds(256 * part + o, 32, stride=8), :] = pieces[o]
    rows = jnp.concatenate([held_ref[:256, :], held_ref[256:, :]], axis=1)
    out_ref[...] = dot3(rows, plane_waves(freq_ref))


def outer_grads(pieces_ref, tile, p):
    grads = jnp.concatenate(
        [pieces_ref[2 * o, p] + pieces_ref[2 * o + 1, p] for o in range(4)], axis=0
    )
    return mul(jnp.concatenate(split(grads.T), axis=1), tile, NN)


def lift_kernel(pieces_ref, held_modes_ref, weight_ref, small_ref, sum_ref):
    tile = jnp.where(iota((32, 128), 0) == iota((32, 128), 1) % 32, SCALE, 0.0).astype(BF16)
    tile = jnp.concatenate([tile, tile], axis=0)
    even = iota((8, 128), 0) % 2 == 0
    total = [[jnp.zeros((8, 128), F32)] * 2 for channel in range(3)]
    for p in range(4):
        outer = outer_grads(pieces_ref, tile, p)
        real, imag = outer[:64], outer[64:]
        turned = held_modes_ref[8 * p : 8 * p + 8, :].T
        pairs = []
        for channel in range(3):
            first = turned[:64, channel : channel + 1]
            second = turned[64:, channel : channel + 1]
            pairs.append((first * real + second * imag, first * imag - second * real))
        for q in range(32):
            rows = [
                [weight_ref[pl.ds(512 * (4 * part + p) + 16 * q + 8 * k, 8), :] for k in range(2)]
                for part in range(2)
            ]
            for channel in range(3):
                for part in range(2):
                    pair = pairs[channel][part]
                    both = jnp.where(even, pair[q : q + 1], pair[32 + q : 33 + q])
                    for k in range(2):
                        total[channel][k] = total[channel][k] + both * rows[part][k]
    lane = iota((128, 128), 1)
    gather = jnp.where((lane >= 64) & (lane < 96) & (lane % 4 == iota((128, 128), 0) // 32), 1.0, 0.0)
    owner = (iota((16, 128), 1) - 64) // 4 == iota((16, 128), 0) // 2
    lines = []
    for channel in range(3):
        lines.append(
            jnp.sum(
                jnp.where(owner, dot3(jnp.concatenate(total[channel], axis=0), gather), 0.0),
                axis=0,
                keepdims=True,
            )
        )
    total = small_ref[...] + jnp.concatenate(lines + [jnp.zeros((5, 128), F32)], axis=0)
    total = jnp.where(iota((8, 128), 0) < 4, total, pltpu.roll(total, 4, 0))
    for target in range(64):
        sum_ref[8 * target : 8 * target + 8, :] = total


def grad_kernel(pieces_ref, held_modes_ref, lift_ref, grad_ref):
    lift = lift_spread(lift_ref)
    tile = fold_table()
    tile = jnp.concatenate([tile, tile], axis=0)
    for p in range(4):
        spread = spread_modes(held_modes_ref[8 * p : 8 * p + 8, :], lift)
        outer = outer_grads(pieces_ref, tile, p)
        real, imag = spread[:64], spread[64:]
        grad_real, grad_imag = outer[:64], outer[64:]
        results = (real * grad_real + imag * grad_imag, real * grad_imag - imag * grad_real)
        for part in range(2):
            base = 512 * (4 * part + p)
            for r in range(2):
                for k in range(8):
                    grad_ref[pl.ds(base + 2 * k + r, 32, stride=16), :] = results[part][
                        32 * r : 32 * r + 32, 128 * k : 128 * k + 128
                    ]


def last_kernel(sum_ref, lift_ref, mix_ref, lift_out, mix_out, proj_out):
    total = jnp.concatenate([sum_ref[...], jnp.zeros((124, 128), F32)], axis=0) * SCALE
    cross = total[:8, :32]
    turned = total.T[:32]
    mixed = turned[:, 0:1] * lift_ref[0:1]
    for channel in (1, 2):
        mixed = mixed + turned[:, channel : channel + 1] * lift_ref[channel : channel + 1]
    mix_out[...] = mixed
    lift_out[...] = (dot3(cross, mix_ref[...]) + total[:8, 64:96])[:3]
    proj_out[...] = total[:3, 32:64]


def call(kernel, shapes, scratch=(), places=None, name=None):
    specs = {}
    if places is not None:
        specs["out_specs"] = tuple(pl.BlockSpec(memory_space=place) for place in places)
    return pl.pallas_call(
        kernel,
        out_shape=shapes,
        scratch_shapes=list(scratch),
        name=name,
        compiler_params=pltpu.CompilerParams(vmem_limit_bytes=48 * 1024 * 1024),
        **specs,
    )


def array(*shape):
    return jax.ShapeDtypeStruct(shape, F32)


def exchange(value, axes):
    return lax.all_to_all(value, axes, split_axis=0, concat_axis=0, tiled=True)


def body(
    input_field,
    target_field,
    row_mask,
    modes,
    lift_weight,
    mix_weight,
    spectral_weight,
    proj_weight,
):
    field = input_field[0]
    target = target_field[0]
    weight = spectral_weight.reshape(2, 4, 32, 2, 8, 128).transpose(0, 1, 2, 4, 3, 5)
    weight = weight.reshape(4096, 128)
    lift_rows = lift_weight.T

    freq, pieces = call(
        input_depth,
        (jax.ShapeDtypeStruct((8, 128), jnp.int32), array(256, 128)),
        name="input_depth",
    )(modes, field)
    pieces = exchange(pieces.reshape(16, 16, 128), "px").reshape(256, 128)
    pieces = call(input_rows, array(64, 128), name="input_rows")(freq, pieces)
    pieces = exchange(pieces.reshape(8, 8, 128), "py").reshape(64, 128)
    held_modes, pieces = call(
        mix_kernel,
        (array(32, 128), array(8, 4, 8, 128)),
        [pltpu.VMEM((64, 256), F32)],
        name="mix",
    )(freq, pieces, lift_rows, weight)
    pieces = exchange(pieces, "py").reshape(256, 128)
    pieces, mark = call(
        expand,
        (array(2048, 128), array(8, 128)),
        [
            pltpu.VMEM((512, 128), F32),
            pltpu.VMEM((2048, 128), F32),
            pltpu.SemaphoreType.DMA((4,)),
        ],
        (pltpu.HBM, pltpu.VMEM),
        name="expand",
    )(freq, pieces)
    point, proj, mask = call(
        tables_kernel, (array(64, 512), array(128, 512), array(8, 128)), name="tables"
    )(mark, row_mask, lift_rows, mix_weight, proj_weight)
    pieces = exchange(pieces.reshape(128, 16, 128), ("py", "px")).reshape(2048, 128)
    pieces, point_grad, proj_grad = call(
        grid_kernel, (array(2048, 128), array(64, 512), array(64, 512)), name="grid"
    )(freq, pieces, field, target, mask, point, proj)
    small = call(pick_kernel, array(8, 128), name="pick")(point_grad, proj_grad)
    pieces = exchange(pieces.reshape(128, 16, 128), ("py", "px")).reshape(2048, 128)
    pieces = call(reduce_kernel, array(256, 128), [pltpu.VMEM((512, 128), F32)], name="reduce")(
        freq, pieces
    )
    pieces = exchange(pieces.reshape(8, 4, 8, 128), "py")
    sums = call(lift_kernel, array(512, 128), name="lift")(pieces, held_modes, weight, small)
    grad = call(grad_kernel, array(4096, 128), name="grad")(pieces, held_modes, lift_rows)
    sums = exchange(sums.reshape(128, 4, 128), ("px", "py"))
    sums = jnp.sum(sums, axis=0)
    lift_total, mix_total, proj_total = call(
        last_kernel, (array(3, 32), array(32, 32), array(3, 32)), name="last"
    )(sums, lift_rows, mix_weight)
    grad = grad.reshape(2, 4, 32, 8, 2, 128).transpose(0, 1, 2, 4, 3, 5)
    return lift_total.T, mix_total, proj_total, grad.reshape(spectral_weight.shape)


def solution(mesh):
    in_specs = (
        P(None, None, "px", "py", None),
        P(None, None, "px", "py", None),
        P(("seed", "px"), "py"),
        P("seed", None),
        P("seed", None),
        P("seed", None),
        P("seed", "py", None, "px", None),
        P("seed", None),
    )
    out_specs = (
        P("seed", None),
        P("seed", None),
        P("seed", None),
        P("seed", "py", None, "px", None),
    )
    return jax.shard_map(body, mesh=mesh, in_specs=in_specs, out_specs=out_specs, check_vma=False)
```

```python
import math

import jax
import jax.numpy as jnp
from jax import lax
from jax.experimental import pallas as pl
from jax.experimental.pallas import tpu as pltpu
from jax.sharding import PartitionSpec as P

C = 32
N = 128
M = 32
F32 = jnp.float32
BF16 = jnp.bfloat16
SCALE = 1.0 / float(N**3)
GELU_A = math.sqrt(2.0 / math.pi)
GELU_B = 0.044715

NN = (((1,), (0,)), ((), ()))
NT = (((1,), (1,)), ((), ()))


def split(value):
    high = value.astype(BF16)
    return high, (value - high.astype(F32)).astype(BF16)


def mul(left, right, dims):
    return lax.dot_general(left, right, dims, preferred_element_type=F32)


def dot3(left, right, dims=NN):
    left_high, left_low = left if isinstance(left, tuple) else split(left)
    right_high, right_low = right if isinstance(right, tuple) else split(right)
    return (
        mul(left_low, right_high, dims)
        + mul(left_high, right_low, dims)
        + mul(left_high, right_high, dims)
    )


def iota(shape, axis):
    return lax.broadcasted_iota(jnp.int32, shape, axis)


def wave(turns):
    place = jnp.abs((turns & (N - 1)) - N // 2).astype(F32)
    angle = (place - N / 4) * (2.0 * math.pi / N)
    square = angle * angle
    series = 1.0 / 39916800.0
    for term in (362880.0, 5040.0, 120.0, 6.0, 1.0):
        series = 1.0 / term - square * series
    return angle * series


def dot2k(left, right):
    left_high, left_low = split(left)
    right_high, right_low = right if isinstance(right, tuple) else split(right)
    wide = jnp.concatenate([left_high, left_low], axis=1)
    tall = jnp.concatenate([right_high, right_high], axis=0)
    return mul(left_high, right_low, NN) + mul(wide, tall, NN)


def frequency_rows(modes):
    place = iota((M, 128), 1)
    slot = iota((M, 128), 0)
    modes = modes.astype(F32).astype(BF16)
    orders = (
        (0, place % 32),
        (1, place % 32),
        (2, 2 * (place // 2 % 16) + place // 32 % 2),
        (0, 4 * (place // 8 % 8) + place % 4),
    )
    rows = []
    for dim, order in orders:
        pick = jnp.where(slot == order, 1.0, 0.0).astype(BF16)
        rows.append(mul(modes, pick, NN)[dim : dim + 1])
    return jnp.concatenate(rows + rows, axis=0).astype(jnp.int32)


def regroup(pieces):
    group = iota(pieces[0].shape, 1) // 16
    out = []
    for target in range(8):
        total = pieces[target]
        for source in range(8):
            if source != target:
                moved = pltpu.roll(pieces[source], (16 * (source - target)) % 128, 1)
                total = jnp.where(group == source, moved, total)
        out.append(total)
    return out


def depth_waves(freq):
    shape = (N, 128)
    return wave(iota(shape, 0) * freq + 32 * (iota(shape, 1) & 1))


def input_depth(modes_ref, field_ref, freq_ref, out_ref):
    freq = frequency_rows(modes_ref[...])
    freq_ref[...] = freq
    table = split(depth_waves(freq[2:3]).T[:64])
    lane = iota((32, 128), 1)
    blank = jnp.zeros((16, N), F32)
    for x in range(8):
        rows = [field_ref[channel, x] for channel in range(3)] + [blank]
        both = jnp.concatenate(rows + rows, axis=0)
        result = dot3(table, both, NT)
        out_ref[pl.ds(x, 32, stride=8), :] = jnp.where(lane < 64, result[:32], result[32:])


def rows_waves(freq_row, phase):
    shape = (256, 128)
    row = iota(shape, 0)
    place = (row // 16) * 8 + row % 8
    return place * freq_row + phase(row // 8 % 2)


def input_rows(freq_ref, pieces_ref, out_ref):
    lane = iota((256, 128), 1)
    table = wave(rows_waves(freq_ref[3:4, :], lambda part: 32 * ((lane // 4) % 2 - part)))
    out_ref[...] = dot3(table.T[:64], pieces_ref[...])


def weight_rows(weight_ref, part, p):
    base = 512 * (4 * part + p)
    return jnp.concatenate(
        [
            jnp.concatenate(
                [weight_ref[pl.ds(base + 2 * k + r, 32, stride=16), :] for k in range(8)], axis=1
            )
            for r in range(2)
        ],
        axis=0,
    )


def lift_spread(lift_ref):
    pick = jnp.where(iota((32, 1024), 0) == iota((32, 1024), 1) // 32, 1.0, 0.0).astype(BF16)
    high, low = split(lift_ref[...])
    return mul(low, pick, NN) + mul(high, pick, NN)


def spread_modes(modes, lift):
    turned = modes.T
    total = turned[:, 0:1] * lift[0:1]
    for channel in (1, 2):
        total = total + turned[:, channel : channel + 1] * lift[channel : channel + 1]
    return total


def fold_table():
    return jnp.where(iota((32, 1024), 0) == iota((32, 1024), 1) % 32, SCALE, 0.0).astype(BF16)


def mix_kernel(freq_ref, pieces_ref, lift_ref, weight_ref, held_modes_ref, out_ref, held_ref):
    pieces = [pieces_ref[8 * source : 8 * source + 8, :] for source in range(8)]
    rows = split(jnp.concatenate(regroup(pieces), axis=0))
    shape = (N, 128)
    lane = iota(shape, 1)
    turns = iota(shape, 0) * freq_ref[1:2, :]
    held_ref[:, :128] = dot3(rows, wave(turns + 32 * (lane // 64)))
    held_ref[:, 128:] = dot3(rows, wave(turns + 32 * (lane // 64) - 32))
    first_slot = iota((4, 128), 1) // 32 % 2 == 0
    held_modes_ref[...] = jnp.zeros((32, 128), F32)
    for channel in range(3):
        both = []
        for parity in range(2):
            base = 8 * (4 * parity + channel)
            both.append(held_ref[base : base + 4, :128] + held_ref[base + 4 : base + 8, 128:])
        held_modes_ref[pl.ds(channel, 4, stride=8), :] = jnp.where(first_slot, both[0], both[1])
    lift = lift_spread(lift_ref)
    fold = fold_table()
    for p in range(4):
        spread = spread_modes(held_modes_ref[8 * p : 8 * p + 8, :], lift)
        real, imag = spread[:64], spread[64:]
        first, second = weight_rows(weight_ref, 0, p), weight_rows(weight_ref, 1, p)
        product = jnp.concatenate([first * real - second * imag, second * real + first * imag], axis=0)
        high, low = split(product)
        mixed = mul(fold, low, NT) + mul(fold, high, NT)
        for target in range(8):
            start = 8 * (target // 2)
            out_ref[target, p] = mixed[start : start + 8]


def plane_waves(freq_ref):
    shape = (256, 128)
    row, lane = iota(shape, 0), iota(shape, 1)
    table = wave((row % 128) * freq_ref[1:2, :] + 32 * (lane // 64 - row // 128))
    parity = lax.axis_index("py") % 2
    return split(jnp.where(lane // 32 % 2 == parity, table, 0.0))


def expand(freq_ref, pieces_ref, out_hbm, mark_ref, held_ref, out_ref, sems):
    result = dot3(pieces_ref[...], plane_waves(freq_ref), NT)
    held_ref[:256, :] = result[:, :128]
    held_ref[256:, :] = result[:, 128:]
    parts = []
    for part in range(2):
        parts.append(
            regroup([held_ref[pl.ds(256 * part + o, 32, stride=8), :] for o in range(8)])
        )
    lane = iota((256, 128), 1)
    table = wave(rows_waves(freq_ref[0:1, :], lambda part: 32 * (lane // 32 % 2 - part)))
    high = table.astype(BF16)
    both = jnp.where(lane < 64, high.astype(F32), table - high.astype(F32)).astype(BF16)
    high = high[:, :64]
    copies = []
    for pair in range(4):
        wide = jnp.concatenate(
            [
                jnp.concatenate([parts[part][2 * pair + k] for part in range(2)], axis=0)
                for k in range(2)
            ],
            axis=1,
        )
        wide_high, wide_low = split(wide)
        result = mul(high, wide_low, NN) + mul(
            both, jnp.concatenate([wide_high, wide_high], axis=0), NN
        )
        for k in range(2):
            start = 256 * (2 * pair + k)
            out_ref[start : start + 256, :] = result[:, 128 * k : 128 * k + 128]
        rows = pl.ds(512 * pair, 512)
        copies.append(
            pltpu.make_async_copy(out_ref.at[rows, :], out_hbm.at[rows, :], sems.at[pair])
        )
        copies[pair].start()
    mark_ref[...] = jnp.zeros((8, 128), F32)
    for copy in copies:
        copy.wait()


def tables_kernel(mark_ref, mask_ref, lift_ref, mix_ref, proj_ref, point_out, proj_out, mask_out):
    pick = jnp.where(iota((32, 512), 0) == iota((32, 512), 1) // 16, 1.0, 0.0).astype(BF16)
    same = iota((64, 512), 0) % 16 == iota((64, 512), 1) % 16
    owner = iota((64, 512), 0) // 16

    def spread(matrix):
        high, low = split(matrix)
        wide = mul(high, pick, NN) + mul(low, pick, NN)
        total = jnp.zeros((64, 512), F32)
        for channel in range(3):
            total = jnp.where(same & (owner == channel), wide[channel : channel + 1], total)
        return total

    point_out[...] = spread(dot3(lift_ref[...], mix_ref[...], NT))
    table = spread(proj_ref[...])
    proj_out[:64] = table
    proj_out[64:] = table
    repeat = jnp.where(iota((16, 128), 0) == iota((16, 128), 1) % 16, 2.0, 0.0).astype(BF16)
    mask = mul(mask_ref[...].astype(F32).astype(BF16), repeat, NN)
    mask_out[...] = mask + 0.0 * mark_ref[...]


def grid_kernel(
    freq_ref, pieces_ref, field_ref, target_ref, mask_ref, point_ref, proj_ref,
    out_ref, point_grad, proj_grad,
):
    waves = depth_waves(freq_ref[2:3, :]).T[:64]
    point = point_ref[...]
    proj = split(proj_ref[...])
    back = jnp.concatenate(
        [proj[0], proj[1][:64], jnp.zeros((64, 512), BF16)], axis=0
    )
    lower = iota((N, 128), 1) < 64
    blank = jnp.zeros((16, N), F32)
    point_grad[...] = jnp.zeros_like(point_grad)
    proj_grad[...] = jnp.zeros_like(proj_grad)

    def plane(x, carry):
        rows = [field_ref[channel, x] for channel in range(3)] + [blank]
        stack = jnp.concatenate([waves] + rows, axis=0)
        aims = [target_ref[channel, x] for channel in range(3)] + [blank]
        aim = jnp.concatenate(aims + aims, axis=0).T
        coefs = [pieces_ref[pl.ds(512 * o + x, 64, stride=8), :] for o in range(4)]
        coefs = jnp.concatenate([jnp.concatenate(coefs, axis=1), point], axis=0)
        preact = dot2k(stack.T, coefs)
        cube = preact * preact
        bend = jnp.tanh(preact * (GELU_A + (GELU_A * GELU_B) * cube))
        half = 0.5 + 0.5 * bend
        active = split(preact * half)
        slope = half + preact * (0.5 - 0.5 * bend * bend) * (
            GELU_A + (3.0 * GELU_A * GELU_B) * cube
        )
        error = mask_ref[pl.ds(x, 1), :] * (dot3(active, proj, NT) - aim)
        high = error.astype(BF16)
        both = jnp.where(lower, high.astype(F32), error - high.astype(F32)).astype(BF16)
        rate = mul(jnp.concatenate([both, high], axis=1), back, NN) * slope
        both = dot2k(stack, rate)
        for o in range(4):
            out_ref[pl.ds(512 * o + x, 64, stride=8), :] = both[:64, 128 * o : 128 * o + 128]
        point_grad[...] += both[64:]
        proj_grad[...] += dot2k(error.T[:64], active)
        return carry

    lax.fori_loop(0, 8, plane, 0, unroll=8)


def pick_small(point_grad, proj_grad):
    same = iota((64, 512), 0) % 16 == iota((64, 512), 1) % 16
    pick = jnp.where(iota((8, 64), 0) == iota((8, 64), 1) // 16, 1.0, 0.0)
    total = jnp.zeros((8, 128), F32)
    for offset, ref in ((0, point_grad), (32, proj_grad)):
        kept = dot3(pick, jnp.where(same, ref[...], 0.0))
        place = jnp.where(iota((512, 128), 0) // 16 + offset == iota((512, 128), 1), 1.0, 0.0)
        total = total + dot3(kept, place)
    return total


def reduce_kernel(freq_ref, pieces_ref, out_ref, held_ref):
    lane = iota((256, 128), 1)
    table = wave(rows_waves(freq_ref[0:1, :], lambda part: 32 * ((lane // 32) % 2 - part)))
    table = split(table.T[:64])
    results = []
    for j in range(8):
        results.append(dot3(table, pieces_ref[256 * j : 256 * j + 256, :]))
    for part in range(2):
        pieces = regroup([result[32 * part : 32 * part + 32] for result in results])
        for o in range(8):
            held_ref[pl.ds(256 * part + o, 32, stride=8), :] = pieces[o]
    rows = jnp.concatenate([held_ref[:256, :], held_ref[256:, :]], axis=1)
    out_ref[...] = dot3(rows, plane_waves(freq_ref))


def outer_grads(pieces_ref, tile, p):
    grads = jnp.concatenate(
        [pieces_ref[2 * o, p] + pieces_ref[2 * o + 1, p] for o in range(4)], axis=0
    )
    return mul(jnp.concatenate(split(grads.T), axis=1), tile, NN)


def lift_kernel(pieces_ref, held_modes_ref, weight_ref, point_grad, proj_grad, sum_ref):
    tile = jnp.where(iota((32, 128), 0) == iota((32, 128), 1) % 32, SCALE, 0.0).astype(BF16)
    tile = jnp.concatenate([tile, tile], axis=0)
    even = iota((8, 128), 0) % 2 == 0
    total = [[jnp.zeros((8, 128), F32)] * 2 for channel in range(3)]
    for p in range(4):
        outer = outer_grads(pieces_ref, tile, p)
        real, imag = outer[:64], outer[64:]
        turned = held_modes_ref[8 * p : 8 * p + 8, :].T
        pairs = []
        for channel in range(3):
            first = turned[:64, channel : channel + 1]
            second = turned[64:, channel : channel + 1]
            pairs.append((first * real + second * imag, first * imag - second * real))
        for q in range(32):
            rows = [
                [weight_ref[pl.ds(512 * (4 * part + p) + 16 * q + 8 * k, 8), :] for k in range(2)]
                for part in range(2)
            ]
            for channel in range(3):
                for part in range(2):
                    pair = pairs[channel][part]
                    both = jnp.where(even, pair[q : q + 1], pair[32 + q : 33 + q])
                    for k in range(2):
                        total[channel][k] = total[channel][k] + both * rows[part][k]
    lane = iota((128, 128), 1)
    gather = jnp.where((lane >= 64) & (lane < 96) & (lane % 4 == iota((128, 128), 0) // 32), 1.0, 0.0)
    owner = (iota((16, 128), 1) - 64) // 4 == iota((16, 128), 0) // 2
    lines = []
    for channel in range(3):
        lines.append(
            jnp.sum(
                jnp.where(owner, dot3(jnp.concatenate(total[channel], axis=0), gather), 0.0),
                axis=0,
                keepdims=True,
            )
        )
    total = pick_small(point_grad, proj_grad) + jnp.concatenate(lines + [jnp.zeros((5, 128), F32)], axis=0)
    total = jnp.where(iota((8, 128), 0) < 4, total, pltpu.roll(total, 4, 0))
    for target in range(64):
        sum_ref[8 * target : 8 * target + 8, :] = total


def grad_kernel(pieces_ref, held_modes_ref, lift_ref, grad_ref):
    lift = lift_spread(lift_ref)
    tile = fold_table()
    tile = jnp.concatenate([tile, tile], axis=0)
    for p in range(4):
        spread = spread_modes(held_modes_ref[8 * p : 8 * p + 8, :], lift)
        outer = outer_grads(pieces_ref, tile, p)
        real, imag = spread[:64], spread[64:]
        grad_real, grad_imag = outer[:64], outer[64:]
        results = (real * grad_real + imag * grad_imag, real * grad_imag - imag * grad_real)
        for part in range(2):
            base = 512 * (4 * part + p)
            for r in range(2):
                for k in range(8):
                    grad_ref[pl.ds(base + 2 * k + r, 32, stride=16), :] = results[part][
                        32 * r : 32 * r + 32, 128 * k : 128 * k + 128
                    ]


def last_kernel(sum_ref, lift_ref, mix_ref, lift_out, mix_out, proj_out):
    total = jnp.concatenate([sum_ref[...], jnp.zeros((124, 128), F32)], axis=0) * SCALE
    cross = total[:8, :32]
    turned = total.T[:32]
    mixed = turned[:, 0:1] * lift_ref[0:1]
    for channel in (1, 2):
        mixed = mixed + turned[:, channel : channel + 1] * lift_ref[channel : channel + 1]
    mix_out[...] = mixed
    lift_out[...] = (dot3(cross, mix_ref[...]) + total[:8, 64:96])[:3]
    proj_out[...] = total[:3, 32:64]


def call(kernel, shapes, scratch=(), places=None, name=None):
    specs = {}
    if places is not None:
        specs["out_specs"] = tuple(pl.BlockSpec(memory_space=place) for place in places)
    return pl.pallas_call(
        kernel,
        out_shape=shapes,
        scratch_shapes=list(scratch),
        name=name,
        compiler_params=pltpu.CompilerParams(vmem_limit_bytes=48 * 1024 * 1024),
        **specs,
    )


def array(*shape):
    return jax.ShapeDtypeStruct(shape, F32)


def exchange(value, axes):
    return lax.all_to_all(value, axes, split_axis=0, concat_axis=0, tiled=True)


def body(
    input_field,
    target_field,
    row_mask,
    modes,
    lift_weight,
    mix_weight,
    spectral_weight,
    proj_weight,
):
    field = input_field[0]
    target = target_field[0]
    weight = spectral_weight.reshape(2, 4, 32, 2, 8, 128).transpose(0, 1, 2, 4, 3, 5)
    weight = weight.reshape(4096, 128)
    lift_rows = lift_weight.T

    freq, pieces = call(
        input_depth,
        (jax.ShapeDtypeStruct((8, 128), jnp.int32), array(256, 128)),
        name="input_depth",
    )(modes, field)
    pieces = exchange(pieces.reshape(16, 16, 128), "px").reshape(256, 128)
    pieces = call(input_rows, array(64, 128), name="input_rows")(freq, pieces)
    pieces = exchange(pieces.reshape(8, 8, 128), "py").reshape(64, 128)
    held_modes, pieces = call(
        mix_kernel,
        (array(32, 128), array(8, 4, 8, 128)),
        [pltpu.VMEM((64, 256), F32)],
        name="mix",
    )(freq, pieces, lift_rows, weight)
    pieces = exchange(pieces, "py").reshape(256, 128)
    pieces, mark = call(
        expand,
        (array(2048, 128), array(8, 128)),
        [
            pltpu.VMEM((512, 128), F32),
            pltpu.VMEM((2048, 128), F32),
            pltpu.SemaphoreType.DMA((4,)),
        ],
        (pltpu.HBM, pltpu.VMEM),
        name="expand",
    )(freq, pieces)
    point, proj, mask = call(
        tables_kernel, (array(64, 512), array(128, 512), array(8, 128)), name="tables"
    )(mark, row_mask, lift_rows, mix_weight, proj_weight)
    pieces = exchange(pieces.reshape(128, 16, 128), ("py", "px")).reshape(2048, 128)
    pieces, point_grad, proj_grad = call(
        grid_kernel, (array(2048, 128), array(64, 512), array(64, 512)), name="grid"
    )(freq, pieces, field, target, mask, point, proj)
    pieces = exchange(pieces.reshape(128, 16, 128), ("py", "px")).reshape(2048, 128)
    pieces = call(reduce_kernel, array(256, 128), [pltpu.VMEM((512, 128), F32)], name="reduce")(
        freq, pieces
    )
    pieces = exchange(pieces.reshape(8, 4, 8, 128), "py")
    sums = call(lift_kernel, array(512, 128), name="lift")(
        pieces, held_modes, weight, point_grad, proj_grad
    )
    grad = call(grad_kernel, array(4096, 128), name="grad")(pieces, held_modes, lift_rows)
    sums = exchange(sums.reshape(128, 4, 128), ("px", "py"))
    sums = jnp.sum(sums, axis=0)
    lift_total, mix_total, proj_total = call(
        last_kernel, (array(3, 32), array(32, 32), array(3, 32)), name="last"
    )(sums, lift_rows, mix_weight)
    grad = grad.reshape(2, 4, 32, 8, 2, 128).transpose(0, 1, 2, 4, 3, 5)
    return lift_total.T, mix_total, proj_total, grad.reshape(spectral_weight.shape)


def solution(mesh):
    in_specs = (
        P(None, None, "px", "py", None),
        P(None, None, "px", "py", None),
        P(("seed", "px"), "py"),
        P("seed", None),
        P("seed", None),
        P("seed", None),
        P("seed", "py", None, "px", None),
        P("seed", None),
    )
    out_specs = (
        P("seed", None),
        P("seed", None),
        P("seed", None),
        P("seed", "py", None, "px", None),
    )
    return jax.shard_map(body, mesh=mesh, in_specs=in_specs, out_specs=out_specs, check_vma=False)
```

```python
import math

import jax
import jax.numpy as jnp
from jax import lax
from jax.experimental import pallas as pl
from jax.experimental.pallas import tpu as pltpu
from jax.sharding import PartitionSpec as P

C = 32
N = 128
M = 32
F32 = jnp.float32
BF16 = jnp.bfloat16
SCALE = 1.0 / float(N**3)
GELU_A = math.sqrt(2.0 / math.pi)
GELU_B = 0.044715

NN = (((1,), (0,)), ((), ()))
NT = (((1,), (1,)), ((), ()))


def split(value):
    high = value.astype(BF16)
    return high, (value - high.astype(F32)).astype(BF16)


def mul(left, right, dims):
    return lax.dot_general(left, right, dims, preferred_element_type=F32)


def dot3(left, right, dims=NN):
    left_high, left_low = left if isinstance(left, tuple) else split(left)
    right_high, right_low = right if isinstance(right, tuple) else split(right)
    return (
        mul(left_low, right_high, dims)
        + mul(left_high, right_low, dims)
        + mul(left_high, right_high, dims)
    )


def iota(shape, axis):
    return lax.broadcasted_iota(jnp.int32, shape, axis)


def wave(turns):
    place = jnp.abs((turns & (N - 1)) - N // 2).astype(F32)
    angle = (place - N / 4) * (2.0 * math.pi / N)
    square = angle * angle
    series = 1.0 / 39916800.0
    for term in (362880.0, 5040.0, 120.0, 6.0, 1.0):
        series = 1.0 / term - square * series
    return angle * series


def dot2k(left, right):
    left_high, left_low = left if isinstance(left, tuple) else split(left)
    right_high, right_low = right if isinstance(right, tuple) else split(right)
    wide = jnp.concatenate([left_high, left_low], axis=1)
    tall = jnp.concatenate([right_high, right_high], axis=0)
    return mul(left_high, right_low, NN) + mul(wide, tall, NN)


def frequency_rows(modes):
    place = iota((M, 128), 1)
    slot = iota((M, 128), 0)
    modes = modes.astype(F32).astype(BF16)
    orders = (
        (0, place % 32),
        (1, place % 32),
        (2, 2 * (place // 2 % 16) + place // 32 % 2),
        (0, 4 * (place // 8 % 8) + place % 4),
    )
    rows = []
    for dim, order in orders:
        pick = jnp.where(slot == order, 1.0, 0.0).astype(BF16)
        rows.append(mul(modes, pick, NN)[dim : dim + 1])
    return jnp.concatenate(rows + rows, axis=0).astype(jnp.int32)


def regroup(pieces):
    group = iota(pieces[0].shape, 1) // 16
    out = []
    for target in range(8):
        total = pieces[target]
        for source in range(8):
            if source != target:
                moved = pltpu.roll(pieces[source], (16 * (source - target)) % 128, 1)
                total = jnp.where(group == source, moved, total)
        out.append(total)
    return out


def depth_waves(freq):
    shape = (N, 128)
    return wave(iota(shape, 0) * freq + 32 * (iota(shape, 1) & 1))


def input_depth(modes_ref, field_ref, freq_ref, out_ref):
    freq = frequency_rows(modes_ref[...])
    freq_ref[...] = freq
    table = split(depth_waves(freq[2:3]).T[:64])
    lane = iota((32, 128), 1)
    blank = jnp.zeros((16, N), F32)
    for x in range(8):
        rows = [field_ref[channel, x] for channel in range(3)] + [blank]
        both = jnp.concatenate(rows + rows, axis=0)
        result = dot3(table, both, NT)
        out_ref[pl.ds(x, 32, stride=8), :] = jnp.where(lane < 64, result[:32], result[32:])


def rows_waves(freq_row, phase):
    shape = (256, 128)
    row = iota(shape, 0)
    place = (row // 16) * 8 + row % 8
    return place * freq_row + phase(row // 8 % 2)


def input_rows(freq_ref, pieces_ref, out_ref):
    lane = iota((256, 128), 1)
    table = wave(rows_waves(freq_ref[3:4, :], lambda part: 32 * ((lane // 4) % 2 - part)))
    out_ref[...] = dot3(table.T[:64], pieces_ref[...])


def weight_rows(weight_ref, part, p):
    base = 512 * (4 * part + p)
    return jnp.concatenate(
        [
            jnp.concatenate(
                [weight_ref[pl.ds(base + 2 * k + r, 32, stride=16), :] for k in range(8)], axis=1
            )
            for r in range(2)
        ],
        axis=0,
    )


def lift_spread(lift_ref):
    pick = jnp.where(iota((32, 1024), 0) == iota((32, 1024), 1) // 32, 1.0, 0.0).astype(BF16)
    high, low = split(lift_ref[...])
    return mul(low, pick, NN) + mul(high, pick, NN)


def spread_modes(modes, lift):
    turned = modes.T
    total = turned[:, 0:1] * lift[0:1]
    for channel in (1, 2):
        total = total + turned[:, channel : channel + 1] * lift[channel : channel + 1]
    return total


def fold_table():
    return jnp.where(iota((32, 1024), 0) == iota((32, 1024), 1) % 32, SCALE, 0.0).astype(BF16)


def mix_kernel(freq_ref, pieces_ref, lift_ref, weight_ref, held_modes_ref, out_ref, held_ref):
    pieces = [pieces_ref[8 * source : 8 * source + 8, :] for source in range(8)]
    rows = split(jnp.concatenate(regroup(pieces), axis=0))
    shape = (N, 128)
    lane = iota(shape, 1)
    turns = iota(shape, 0) * freq_ref[1:2, :]
    held_ref[:, :128] = dot2k(rows, wave(turns + 32 * (lane // 64)))
    held_ref[:, 128:] = dot2k(rows, wave(turns + 32 * (lane // 64) - 32))
    first_slot = iota((4, 128), 1) // 32 % 2 == 0
    held_modes_ref[...] = jnp.zeros((32, 128), F32)
    for channel in range(3):
        both = []
        for parity in range(2):
            base = 8 * (4 * parity + channel)
            both.append(held_ref[base : base + 4, :128] + held_ref[base + 4 : base + 8, 128:])
        held_modes_ref[pl.ds(channel, 4, stride=8), :] = jnp.where(first_slot, both[0], both[1])
    lift = lift_spread(lift_ref)
    fold = fold_table()
    for p in range(4):
        spread = spread_modes(held_modes_ref[8 * p : 8 * p + 8, :], lift)
        real, imag = spread[:64], spread[64:]
        first, second = weight_rows(weight_ref, 0, p), weight_rows(weight_ref, 1, p)
        product = jnp.concatenate([first * real - second * imag, second * real + first * imag], axis=0)
        high, low = split(product)
        mixed = mul(fold, low, NT) + mul(fold, high, NT)
        for target in range(8):
            start = 8 * (target // 2)
            out_ref[target, p] = mixed[start : start + 8]


def plane_waves(freq_ref):
    shape = (256, 128)
    row, lane = iota(shape, 0), iota(shape, 1)
    table = wave((row % 128) * freq_ref[1:2, :] + 32 * (lane // 64 - row // 128))
    parity = lax.axis_index("py") % 2
    return split(jnp.where(lane // 32 % 2 == parity, table, 0.0))


def expand(freq_ref, pieces_ref, out_hbm, mark_ref, held_ref, out_ref, sems):
    high, low = split(pieces_ref[...])
    table_high, table_low = plane_waves(freq_ref)
    result = mul(high, table_low, NT) + mul(
        jnp.concatenate([high, low], axis=1),
        jnp.concatenate([table_high, table_high], axis=1),
        NT,
    )
    held_ref[:256, :] = result[:, :128]
    held_ref[256:, :] = result[:, 128:]
    parts = []
    for part in range(2):
        parts.append(
            regroup([held_ref[pl.ds(256 * part + o, 32, stride=8), :] for o in range(8)])
        )
    lane = iota((256, 128), 1)
    table = wave(rows_waves(freq_ref[0:1, :], lambda part: 32 * (lane // 32 % 2 - part)))
    high = table.astype(BF16)
    both = jnp.where(lane < 64, high.astype(F32), table - high.astype(F32)).astype(BF16)
    high = high[:, :64]
    copies = []
    for pair in range(4):
        wide = jnp.concatenate(
            [
                jnp.concatenate([parts[part][2 * pair + k] for part in range(2)], axis=0)
                for k in range(2)
            ],
            axis=1,
        )
        wide_high, wide_low = split(wide)
        result = mul(high, wide_low, NN) + mul(
            both, jnp.concatenate([wide_high, wide_high], axis=0), NN
        )
        for k in range(2):
            start = 256 * (2 * pair + k)
            out_ref[start : start + 256, :] = result[:, 128 * k : 128 * k + 128]
        rows = pl.ds(512 * pair, 512)
        copies.append(
            pltpu.make_async_copy(out_ref.at[rows, :], out_hbm.at[rows, :], sems.at[pair])
        )
        copies[pair].start()
    mark_ref[...] = jnp.zeros((8, 128), F32)
    for copy in copies:
        copy.wait()


def tables_kernel(mark_ref, mask_ref, lift_ref, mix_ref, proj_ref, point_out, proj_out, mask_out):
    pick = jnp.where(iota((32, 512), 0) == iota((32, 512), 1) // 16, 1.0, 0.0).astype(BF16)
    same = iota((64, 512), 0) % 16 == iota((64, 512), 1) % 16
    owner = iota((64, 512), 0) // 16

    def spread(matrix):
        high, low = split(matrix)
        wide = mul(high, pick, NN) + mul(low, pick, NN)
        total = jnp.zeros((64, 512), F32)
        for channel in range(3):
            total = jnp.where(same & (owner == channel), wide[channel : channel + 1], total)
        return total

    point_out[...] = spread(dot3(lift_ref[...], mix_ref[...], NT))
    table = spread(proj_ref[...])
    proj_out[:64] = table
    proj_out[64:] = table
    repeat = jnp.where(iota((16, 128), 0) == iota((16, 128), 1) % 16, 2.0, 0.0).astype(BF16)
    mask = mul(mask_ref[...].astype(F32).astype(BF16), repeat, NN)
    mask_out[...] = mask + 0.0 * mark_ref[...]


def grid_kernel(
    freq_ref, pieces_ref, field_ref, target_ref, mask_ref, point_ref, proj_ref,
    out_ref, point_grad, proj_grad,
):
    waves = depth_waves(freq_ref[2:3, :]).T[:64]
    point = point_ref[...]
    proj = split(proj_ref[...])
    back = jnp.concatenate(
        [proj[0], proj[1][:64], jnp.zeros((64, 512), BF16)], axis=0
    )
    lower = iota((N, 128), 1) < 64
    blank = jnp.zeros((16, N), F32)
    point_grad[...] = jnp.zeros_like(point_grad)
    proj_grad[...] = jnp.zeros_like(proj_grad)

    def plane(x, carry):
        rows = [field_ref[channel, x] for channel in range(3)] + [blank]
        stack = jnp.concatenate([waves] + rows, axis=0)
        aims = [target_ref[channel, x] for channel in range(3)] + [blank]
        aim = jnp.concatenate(aims + aims, axis=0).T
        coefs = [pieces_ref[pl.ds(512 * o + x, 64, stride=8), :] for o in range(4)]
        coefs = jnp.concatenate([jnp.concatenate(coefs, axis=1), point], axis=0)
        preact = dot2k(stack.T, coefs)
        cube = preact * preact
        bend = jnp.tanh(preact * (GELU_A + (GELU_A * GELU_B) * cube))
        half = 0.5 + 0.5 * bend
        active = split(preact * half)
        slope = half + preact * (0.5 - 0.5 * bend * bend) * (
            GELU_A + (3.0 * GELU_A * GELU_B) * cube
        )
        error = mask_ref[pl.ds(x, 1), :] * (dot3(active, proj, NT) - aim)
        high = error.astype(BF16)
        both = jnp.where(lower, high.astype(F32), error - high.astype(F32)).astype(BF16)
        rate = mul(jnp.concatenate([both, high], axis=1), back, NN) * slope
        both = dot2k(stack, rate)
        for o in range(4):
            out_ref[pl.ds(512 * o + x, 64, stride=8), :] = both[:64, 128 * o : 128 * o + 128]
        point_grad[...] += both[64:]
        proj_grad[...] += dot2k(error.T[:64], active)
        return carry

    lax.fori_loop(0, 8, plane, 0, unroll=8)


def pick_small(point_grad, proj_grad):
    same = iota((64, 512), 0) % 16 == iota((64, 512), 1) % 16
    pick = jnp.where(iota((8, 64), 0) == iota((8, 64), 1) // 16, 1.0, 0.0)
    total = jnp.zeros((8, 128), F32)
    for offset, ref in ((0, point_grad), (32, proj_grad)):
        kept = dot3(pick, jnp.where(same, ref[...], 0.0))
        place = jnp.where(iota((512, 128), 0) // 16 + offset == iota((512, 128), 1), 1.0, 0.0)
        total = total + dot3(kept, place)
    return total


def reduce_kernel(freq_ref, pieces_ref, out_ref, held_ref):
    lane = iota((256, 128), 1)
    table = wave(rows_waves(freq_ref[0:1, :], lambda part: 32 * ((lane // 32) % 2 - part)))
    table = split(table.T[:64])
    results = []
    for j in range(8):
        results.append(dot3(table, pieces_ref[256 * j : 256 * j + 256, :]))
    for part in range(2):
        pieces = regroup([result[32 * part : 32 * part + 32] for result in results])
        for o in range(8):
            held_ref[pl.ds(256 * part + o, 32, stride=8), :] = pieces[o]
    rows = jnp.concatenate([held_ref[:256, :], held_ref[256:, :]], axis=1)
    out_ref[...] = dot3(rows, plane_waves(freq_ref))


def outer_grads(pieces_ref, tile, p):
    grads = jnp.concatenate(
        [pieces_ref[2 * o, p] + pieces_ref[2 * o + 1, p] for o in range(4)], axis=0
    )
    return mul(jnp.concatenate(split(grads.T), axis=1), tile, NN)


def lift_kernel(pieces_ref, held_modes_ref, weight_ref, point_grad, proj_grad, sum_ref):
    tile = jnp.where(iota((32, 128), 0) == iota((32, 128), 1) % 32, SCALE, 0.0).astype(BF16)
    tile = jnp.concatenate([tile, tile], axis=0)
    even = iota((8, 128), 0) % 2 == 0
    total = [[jnp.zeros((8, 128), F32)] * 2 for channel in range(3)]
    for p in range(4):
        outer = outer_grads(pieces_ref, tile, p)
        real, imag = outer[:64], outer[64:]
        turned = held_modes_ref[8 * p : 8 * p + 8, :].T
        pairs = []
        for channel in range(3):
            first = turned[:64, channel : channel + 1]
            second = turned[64:, channel : channel + 1]
            pairs.append((first * real + second * imag, first * imag - second * real))
        for q in range(32):
            rows = [
                [weight_ref[pl.ds(512 * (4 * part + p) + 16 * q + 8 * k, 8), :] for k in range(2)]
                for part in range(2)
            ]
            for channel in range(3):
                for part in range(2):
                    pair = pairs[channel][part]
                    both = jnp.where(even, pair[q : q + 1], pair[32 + q : 33 + q])
                    for k in range(2):
                        total[channel][k] = total[channel][k] + both * rows[part][k]
    lane = iota((128, 128), 1)
    gather = jnp.where((lane >= 64) & (lane < 96) & (lane % 4 == iota((128, 128), 0) // 32), 1.0, 0.0)
    owner = (iota((16, 128), 1) - 64) // 4 == iota((16, 128), 0) // 2
    lines = []
    for channel in range(3):
        lines.append(
            jnp.sum(
                jnp.where(owner, dot3(jnp.concatenate(total[channel], axis=0), gather), 0.0),
                axis=0,
                keepdims=True,
            )
        )
    total = pick_small(point_grad, proj_grad) + jnp.concatenate(lines + [jnp.zeros((5, 128), F32)], axis=0)
    total = jnp.where(iota((8, 128), 0) < 4, total, pltpu.roll(total, 4, 0))
    for target in range(64):
        sum_ref[8 * target : 8 * target + 8, :] = total


def grad_kernel(pieces_ref, held_modes_ref, lift_ref, grad_ref):
    lift = lift_spread(lift_ref)
    tile = fold_table()
    tile = jnp.concatenate([tile, tile], axis=0)
    for p in range(4):
        spread = spread_modes(held_modes_ref[8 * p : 8 * p + 8, :], lift)
        outer = outer_grads(pieces_ref, tile, p)
        real, imag = spread[:64], spread[64:]
        grad_real, grad_imag = outer[:64], outer[64:]
        results = (real * grad_real + imag * grad_imag, real * grad_imag - imag * grad_real)
        for part in range(2):
            base = 512 * (4 * part + p)
            for r in range(2):
                for k in range(8):
                    grad_ref[pl.ds(base + 2 * k + r, 32, stride=16), :] = results[part][
                        32 * r : 32 * r + 32, 128 * k : 128 * k + 128
                    ]


def last_kernel(sum_ref, lift_ref, mix_ref, lift_out, mix_out, proj_out):
    total = jnp.concatenate([sum_ref[...], jnp.zeros((124, 128), F32)], axis=0) * SCALE
    cross = total[:8, :32]
    turned = total.T[:32]
    mixed = turned[:, 0:1] * lift_ref[0:1]
    for channel in (1, 2):
        mixed = mixed + turned[:, channel : channel + 1] * lift_ref[channel : channel + 1]
    mix_out[...] = mixed
    lift_out[...] = (dot3(cross, mix_ref[...]) + total[:8, 64:96])[:3]
    proj_out[...] = total[:3, 32:64]


def call(kernel, shapes, scratch=(), places=None, name=None):
    specs = {}
    if places is not None:
        specs["out_specs"] = tuple(pl.BlockSpec(memory_space=place) for place in places)
    return pl.pallas_call(
        kernel,
        out_shape=shapes,
        scratch_shapes=list(scratch),
        name=name,
        compiler_params=pltpu.CompilerParams(vmem_limit_bytes=48 * 1024 * 1024),
        **specs,
    )


def array(*shape):
    return jax.ShapeDtypeStruct(shape, F32)


def exchange(value, axes):
    return lax.all_to_all(value, axes, split_axis=0, concat_axis=0, tiled=True)


def body(
    input_field,
    target_field,
    row_mask,
    modes,
    lift_weight,
    mix_weight,
    spectral_weight,
    proj_weight,
):
    field = input_field[0]
    target = target_field[0]
    weight = spectral_weight.reshape(2, 4, 32, 2, 8, 128).transpose(0, 1, 2, 4, 3, 5)
    weight = weight.reshape(4096, 128)
    lift_rows = lift_weight.T

    freq, pieces = call(
        input_depth,
        (jax.ShapeDtypeStruct((8, 128), jnp.int32), array(256, 128)),
        name="input_depth",
    )(modes, field)
    pieces = exchange(pieces.reshape(16, 16, 128), "px").reshape(256, 128)
    pieces = call(input_rows, array(64, 128), name="input_rows")(freq, pieces)
    pieces = exchange(pieces.reshape(8, 8, 128), "py").reshape(64, 128)
    held_modes, pieces = call(
        mix_kernel,
        (array(32, 128), array(8, 4, 8, 128)),
        [pltpu.VMEM((64, 256), F32)],
        name="mix",
    )(freq, pieces, lift_rows, weight)
    pieces = exchange(pieces, "py").reshape(256, 128)
    pieces, mark = call(
        expand,
        (array(2048, 128), array(8, 128)),
        [
            pltpu.VMEM((512, 128), F32),
            pltpu.VMEM((2048, 128), F32),
            pltpu.SemaphoreType.DMA((4,)),
        ],
        (pltpu.HBM, pltpu.VMEM),
        name="expand",
    )(freq, pieces)
    point, proj, mask = call(
        tables_kernel, (array(64, 512), array(128, 512), array(8, 128)), name="tables"
    )(mark, row_mask, lift_rows, mix_weight, proj_weight)
    pieces = exchange(pieces.reshape(128, 16, 128), ("py", "px")).reshape(2048, 128)
    pieces, point_grad, proj_grad = call(
        grid_kernel, (array(2048, 128), array(64, 512), array(64, 512)), name="grid"
    )(freq, pieces, field, target, mask, point, proj)
    pieces = exchange(pieces.reshape(128, 16, 128), ("py", "px")).reshape(2048, 128)
    pieces = call(reduce_kernel, array(256, 128), [pltpu.VMEM((512, 128), F32)], name="reduce")(
        freq, pieces
    )
    pieces = exchange(pieces.reshape(8, 4, 8, 128), "py")
    sums = call(lift_kernel, array(512, 128), name="lift")(
        pieces, held_modes, weight, point_grad, proj_grad
    )
    grad = call(grad_kernel, array(4096, 128), name="grad")(pieces, held_modes, lift_rows)
    sums = exchange(sums.reshape(128, 4, 128), ("px", "py"))
    sums = jnp.sum(sums, axis=0)
    lift_total, mix_total, proj_total = call(
        last_kernel, (array(3, 32), array(32, 32), array(3, 32)), name="last"
    )(sums, lift_rows, mix_weight)
    grad = grad.reshape(2, 4, 32, 8, 2, 128).transpose(0, 1, 2, 4, 3, 5)
    return lift_total.T, mix_total, proj_total, grad.reshape(spectral_weight.shape)


def solution(mesh):
    in_specs = (
        P(None, None, "px", "py", None),
        P(None, None, "px", "py", None),
        P(("seed", "px"), "py"),
        P("seed", None),
        P("seed", None),
        P("seed", None),
        P("seed", "py", None, "px", None),
        P("seed", None),
    )
    out_specs = (
        P("seed", None),
        P("seed", None),
        P("seed", None),
        P("seed", "py", None, "px", None),
    )
    return jax.shard_map(body, mesh=mesh, in_specs=in_specs, out_specs=out_specs, check_vma=False)
```
